768 devices in a mesh: pipe: 2 (over core), dp: 48 (over z, x), tensor: 8 (over y).
Axes of the slice: x: 4, y: 8, z: 12, core: 2. Of those that a mesh axis runs over, the one named last changes fastest.
Arguments:
- stream_in: bfloat16 [2, 24576, 4096], P('pipe', 'dp', 'tensor'), may hold values from -4.5 to 4.5
- saved_in: bfloat16 [2, 24576, 4096], P('pipe', 'dp', 'tensor'), may hold values from -4.5 to 4.5
- grad_out: bfloat16 [2, 24576, 4096], P('pipe', 'dp', 'tensor'), may hold values from -6 to 6
- mem_keys: bfloat16 [2, 96, 8, 4096], P('pipe', 'dp', None, 'tensor'), may hold values from -4.5 to 4.5
- mem_values: bfloat16 [2, 96, 8, 4096], P('pipe', 'dp', None, 'tensor'), may hold values from -6 to 6
- owner_map: int32 [96], replicated, may hold values from 0 to 95, as said below
- block_ids: int32 [2, 2, 48, 16], P(None, 'pipe', 'dp'), may hold values from 0 to 95, as said below
Outputs:
- next_input: bfloat16 [2, 24576, 4096], P('pipe', 'dp', 'tensor')
- grad_back: bfloat16 [2, 24576, 4096], P('pipe', 'dp', 'tensor')
- key_grad: bfloat16 [2, 96, 8, 4096], P('pipe', 'dp', None, 'tensor')
- value_grad: bfloat16 [2, 96, 8, 4096], P('pipe', 'dp', None, 'tensor')
The draws below stay inside these ranges and needn't reach their ends.
Inputs may be any that keep to these rules, and one draw needn't show every extreme that they name: `owner_map`: A permutation of the block ids; location loc lies with replica loc // 2 in slot loc % 2. `block_ids`: for each section and replica, the 32 ids of both micro-batches together lie with 32 different replicas, so at most one block is requested from one replica; in every section one replica is asked for a block by every replica, itself included.
All inputs are finite; a program needn't handle non-finite values.
Results may differ from the reference program's by a relative error of at most 0.0057.
Values may be sent and summed in bfloat16 or wider, within the bound.
A program may use at most 32 MiB of HBM per device.

```python
import math
import jax
import jax.numpy as jnp
from jax import lax

HEAD_DIM = 128
MEM_BLK = 8
TOK_DEV = 512
MB_DEV = 2
TOPK = 16
SECTIONS = 2
TOKENS = 24576
FEATURES = 4096
MEM_BLOCKS = 96
N_DP = 48


def activation(key, code):
    local = jax.random.fold_in(key, code)
    shape = (SECTIONS, TOKENS, FEATURES)
    result = jnp.clip(jax.random.normal(local, shape, jnp.float32), -4.5, 4.5)
    return result.astype(jnp.bfloat16)


def draw_stream_in(key, part):
    return activation(key, 1)


def draw_saved_in(key, part):
    return activation(key, 2)


def draw_mem_keys(key, part):
    local = jax.random.fold_in(key, 3)
    shape = (SECTIONS, MEM_BLOCKS, MEM_BLK, FEATURES)
    result = jnp.clip(jax.random.normal(local, shape, jnp.float32), -4.5, 4.5)
    return result.astype(jnp.bfloat16)


def shared_tables(key):
    base = jax.random.fold_in(key, 5)
    owner_map = jax.random.permutation(jax.random.fold_in(base, 0), MEM_BLOCKS).astype(jnp.int32)
    holder = jnp.argsort(owner_map).astype(jnp.int32)
    replicas = MEM_BLOCKS // MB_DEV
    total_rows = SECTIONS * replicas
    row_keys = jax.random.split(jax.random.fold_in(base, 1), total_rows)
    hot = jax.random.randint(jax.random.fold_in(base, 3), (SECTIONS,), 0, replicas).astype(jnp.int32)
    hot_rows = jnp.repeat(hot, replicas)

    def pick_row(row_key, hot_one):
        others = jax.random.permutation(row_key, replicas - 1)[:2 * TOPK - 1].astype(jnp.int32)
        others = others + (others >= hot_one).astype(jnp.int32)
        members = jnp.concatenate([hot_one[None], others])
        order = jax.random.permutation(jax.random.fold_in(row_key, 7), 2 * TOPK)
        return members[order].astype(jnp.int32)
    chosen = jax.vmap(pick_row)(row_keys, hot_rows)
    slot_ids = jax.random.randint(jax.random.fold_in(base, 2), (total_rows, 2 * TOPK), 0, MB_DEV)
    places = (chosen * MB_DEV + slot_ids).astype(jnp.int32)
    picked = holder[places].reshape(SECTIONS, replicas, 2, TOPK)
    return (owner_map, jnp.transpose(picked, (2, 0, 1, 3)).astype(jnp.int32))


def draw_owner_map(key, part):
    return shared_tables(key)[0]


def draw_block_ids(key, part):
    return shared_tables(key)[1]


def block_levels(own_key, shape, cuts, least, top_value):
    loudness, own = 1.0, jax.random.fold_in(own_key, 6)
    for axis_at, shards_of in cuts:
        draws = jnp.exp(jax.random.uniform(jax.random.fold_in(own, axis_at), (shards_of,), jnp.float32, least / len(cuts), top_value / len(cuts)))
        loudness = loudness * jnp.repeat(draws, shape[axis_at] // shards_of).reshape([-1 if axis == axis_at else 1 for axis in range(len(shape))])
    return loudness


def bell_draw(stream_key, extent, deviation, limit, cuts=(), dtype=jnp.bfloat16):
    values = jax.random.normal(stream_key, extent, jnp.float32) * deviation
    if len(cuts) > 0:
        values = block_levels(stream_key, extent, cuts, -0.22, 0.18) * values
    return jnp.clip(values, min=-limit, max=limit).astype(dtype)


def setup_inputs(seed: int = 0) -> dict:
    arg_keys = jax.random.split(jax.random.key(seed), 8)
    return {
        "stream_in": draw_stream_in(jax.random.fold_in(arg_keys[7], 71), 0),
        "saved_in": draw_saved_in(jax.random.fold_in(arg_keys[7], 71), 0),
        "grad_out": bell_draw(arg_keys[2], (SECTIONS, TOKENS, FEATURES), 1.0, 6.0, ((0, 2), (1, 48), (2, 8))),
        "mem_keys": draw_mem_keys(jax.random.fold_in(arg_keys[7], 71), 0),
        "mem_values": bell_draw(arg_keys[4], (SECTIONS, MEM_BLOCKS, MEM_BLK, FEATURES), 1.0, 6.0, ((0, 2), (1, 48), (3, 8))),
        "owner_map": draw_owner_map(jax.random.fold_in(arg_keys[7], 71), 0),
        "block_ids": draw_block_ids(jax.random.fold_in(arg_keys[7], 71), 0),
    }


def forward_part(inputs, memory_keys, memory_values):
    rows = inputs.shape[0]
    heads_count = inputs.shape[1] // HEAD_DIM
    scale = 1.0 / math.sqrt(HEAD_DIM)
    queries = inputs.astype(jnp.float32).reshape(rows, heads_count, HEAD_DIM)
    key_rows = memory_keys.astype(jnp.float32).reshape(-1, heads_count, HEAD_DIM)
    value_rows = memory_values.astype(jnp.float32).reshape(-1, heads_count, HEAD_DIM)
    scores = jnp.einsum('thd,khd->htk', queries, key_rows) * scale
    exponent = jnp.exp(scores - lax.optimization_barrier(jnp.max(scores, axis=-1, keepdims=True)))
    weights = exponent / lax.optimization_barrier(jnp.sum(exponent, axis=-1, keepdims=True))
    rounded = lax.optimization_barrier(weights.astype(jnp.bfloat16)).astype(jnp.float32)
    attended = jnp.einsum('htk,khd->thd', rounded, value_rows).reshape(rows, -1)
    return (queries, key_rows, value_rows, weights, rounded, attended)

def backward_part(inputs, grads, memory_keys, memory_values):
    queries, key_rows, value_rows, weights, rounded, attended = forward_part(inputs, memory_keys, memory_values)
    rows = inputs.shape[0]
    heads_count = queries.shape[1]
    scale = 1.0 / math.sqrt(HEAD_DIM)
    grad_rows = grads.astype(jnp.float32).reshape(rows, heads_count, HEAD_DIM)
    grad_weights = jnp.einsum('thd,khd->htk', grad_rows, value_rows)
    centre = lax.optimization_barrier(jnp.sum(weights * grad_weights, axis=-1, keepdims=True))
    grad_scores = weights * (grad_weights - centre) * scale
    grad_scores = lax.optimization_barrier(grad_scores.astype(jnp.bfloat16)).astype(jnp.float32)
    grad_queries = jnp.einsum('htk,khd->thd', grad_scores, key_rows).reshape(rows, -1)
    key_terms = jnp.einsum('htk,thd->khd', grad_scores, queries).reshape(key_rows.shape[0], -1)
    value_terms = jnp.einsum('htk,thd->khd', rounded, grad_rows).reshape(key_rows.shape[0], -1)
    input_grad = (grads.astype(jnp.float32) + grad_queries).astype(jnp.bfloat16)
    return (input_grad, key_terms.astype(jnp.bfloat16), value_terms.astype(jnp.bfloat16))

def reference(stream_in, saved_in, grad_out, mem_keys, mem_values, owner_map, block_ids):
    locations = owner_map[block_ids].astype(jnp.int32)
    width = stream_in.shape[2]

    def section(packed):
        forward_rows, backward_rows, upstream, sec_keys, sec_values, places = packed

        def fetch(where):
            return (sec_keys[where].reshape(TOPK * MEM_BLK, width), sec_values[where].reshape(TOPK * MEM_BLK, width))

        def forward_one(inputs, where):
            fetched_keys, fetched_values = fetch(where)
            attended = forward_part(inputs, fetched_keys, fetched_values)[5]
            return (inputs.astype(jnp.float32) + attended).astype(jnp.bfloat16)

        def backward_one(inputs, grads, where):
            fetched_keys, fetched_values = fetch(where)
            return backward_part(inputs, grads, fetched_keys, fetched_values)
        outputs = jax.vmap(forward_one)(forward_rows.reshape(N_DP, TOK_DEV, width), places[0])
        input_grads, key_terms, value_terms = jax.vmap(backward_one)(backward_rows.reshape(N_DP, TOK_DEV, width), upstream.reshape(N_DP, TOK_DEV, width), places[1])
        flat = places[1].reshape(-1)
        key_total = jnp.zeros((MEM_BLOCKS, MEM_BLK, width), jnp.float32).at[flat].add(key_terms.astype(jnp.float32).reshape(N_DP * TOPK, MEM_BLK, width))
        value_total = jnp.zeros((MEM_BLOCKS, MEM_BLK, width), jnp.float32).at[flat].add(value_terms.astype(jnp.float32).reshape(N_DP * TOPK, MEM_BLK, width))
        return (outputs.reshape(TOKENS, width), input_grads.reshape(TOKENS, width), key_total.astype(jnp.bfloat16), value_total.astype(jnp.bfloat16))
    results = lax.map(section, (stream_in, saved_in, grad_out, mem_keys, mem_values, jnp.moveaxis(locations, 1, 0)))
    blank = jnp.zeros((1, TOKENS, width), jnp.bfloat16)
    next_input = jnp.concatenate([blank, results[0][:-1]], axis=0)
    grad_back = jnp.concatenate([results[1][1:], blank], axis=0)
    return (next_input, grad_back, results[2], results[3])
```

```python
import functools
import math

import jax
import jax.numpy as jnp
from jax import lax
from jax.experimental import pallas as pl
from jax.experimental.pallas import tpu as pltpu
from jax.sharding import PartitionSpec as P

HEAD = 128
X = 4
BF16 = jnp.bfloat16
F32 = jnp.float32
NT = (((1,), (1,)), ((), ()))
TN = (((0,), (0,)), ((), ()))


def wait_for(ref, sem):
    pltpu.make_async_copy(ref, ref, sem).wait()


def kernel(
    Z, blk, picks,
    stream_ref, saved_ref, grad_ref, mk_ref, mv_ref, om_ref, ids_ref,
    next_ref, back_ref, kg_ref, vg_ref,
    stream_v, saved_v, grad_v, mem_v, G, T, onehot, kb, vb, kf, vf, kt, vt, gs, res, zero,
    rkz, rvz, rva, rvb, rkx, om_s, ids_s,
    load_sem, small_sem, agk_x, agk_z, agv_z, agv_x, agv_r, ag_send,
    rsk_z, rsk_x, rsv_a, rsv_b, rsv_z, rs_send, pipe_send, pipe_recv, zero_sem,
):
    pipe, dp, ten = lax.axis_index("pipe"), lax.axis_index("dp"), lax.axis_index("tensor")
    z, x = dp // X, dp % X
    H = Z // 2
    W = stream_v.shape[1]
    heads = W // HEAD
    half = W // 2
    rows = 2 * blk
    scale = 1.0 / math.sqrt(HEAD)

    def at(dz, dx):
        return lax.rem(z + dz + Z, Z) * X + lax.rem(x + dx + X, X)

    def send(src, dst, ssem, rsem, dz, dx):
        pltpu.make_async_remote_copy(
            src_ref=src, dst_ref=dst, send_sem=ssem, recv_sem=rsem,
            device_id=(pipe, at(dz, dx), ten), device_id_type=pl.DeviceIdType.MESH,
        ).start()

    mem_loads = [
        pltpu.make_async_copy(mk_ref, mem_v.at[0], small_sem.at[0]),
        pltpu.make_async_copy(mv_ref, mem_v.at[1], small_sem.at[1]),
    ]
    id_loads = [
        pltpu.make_async_copy(om_ref, om_s, small_sem.at[2]),
        pltpu.make_async_copy(ids_ref, ids_s, small_sem.at[3]),
    ]
    loads = [
        pltpu.make_async_copy(saved_ref, saved_v, load_sem.at[0]),
        pltpu.make_async_copy(grad_ref, grad_v, load_sem.at[1]),
        pltpu.make_async_copy(stream_ref, stream_v, load_sem.at[2]),
    ]
    for copy in mem_loads + id_loads + loads:
        copy.start()

    barrier = pltpu.get_barrier_semaphore()
    for dz, dx in ((1, 0), (-1, 0), (0, 1), (0, 2), (0, 3)):
        pl.semaphore_signal(
            barrier, inc=1, device_id=(pipe, at(dz, dx), ten), device_id_type=pl.DeviceIdType.MESH
        )
    pl.semaphore_signal(
        barrier, inc=1, device_id=(1 - pipe, dp, ten), device_id_type=pl.DeviceIdType.MESH
    )
    for kv in range(2):
        mem_loads[kv].wait()
        own = jnp.concatenate([mem_v[kv, 0].astype(F32), mem_v[kv, 1].astype(F32)], axis=0)
        G[kv, dp] = own.astype(BF16)
    pl.semaphore_wait(barrier, 6)

    halves = (slice(0, half), slice(half, W))
    k_order = (0, 1, 3, 2)
    k_half = ((0, 1), (3, 2))

    def v_to_x(o):
        for d, dx in ((0, 1), (1, -1)):
            ref = G.at[1, at(o, 0)]
            send(ref, ref, ag_send.at[1], agv_x.at[d, o % Z], 0, dx)

    def v_relay(o):
        for d, dx in ((0, 1), (1, -1)):
            wait_for(G.at[1, at(o, -dx)], agv_x.at[d, o % Z])
            ref = G.at[1, at(o, -dx), :, halves[d]]
            send(ref, ref, ag_send.at[1], agv_r.at[d, o % Z], 0, dx)

    def v_relay_wait(o):
        for d in range(2):
            wait_for(G.at[1, at(o, 2), :, halves[d]], agv_r.at[d, o % Z])

    for r in (1, 3, 2):
        ref = G.at[0, dp]
        send(ref, ref, ag_send.at[0], agk_x.at[r - 1], 0, r)
    for d, dz in ((0, 1), (1, -1)):
        ref = G.at[1, dp]
        send(ref, ref, ag_send.at[1], agv_z.at[d, 0], dz, 0)
    v_to_x(0)
    for i, r in enumerate(k_order):
        if r:
            wait_for(G.at[0, at(0, r)], agk_x.at[(X - r) - 1])
        for d, dz in ((0, 1), (1, -1)):
            if H > 1 or r in k_half[d]:
                ref = G.at[0, at(0, r)]
                send(ref, ref, ag_send.at[0], agk_z.at[d, 0, r], dz, 0)

    for copy in id_loads:
        copy.wait()
    places = [[om_s[ids_s[m, 0, 0, j]] for j in range(picks)] for m in range(2)]
    total = Z * X * rows
    ramp = lax.broadcasted_iota(jnp.int32, (blk, total), 1) - lax.broadcasted_iota(
        jnp.int32, (blk, total), 0
    )
    for m in range(2):
        for j in range(0, picks, 2):
            pair = [
                jnp.where(ramp == places[m][i] * blk, 1.0, 0.0).astype(F32) for i in (j, j + 1)
            ]
            onehot[m, j * blk:(j + 2) * blk, :] = jnp.concatenate(pair, axis=0).astype(BF16)

    for s in range(1, H + 1):
        for d, dz in ((0, 1), (1, -1)):
            o = -dz * s
            if s < H:
                ref = G.at[1, at(o, 0)]
                wait_for(ref, agv_z.at[d, s - 1])
                if s + 1 < H:
                    send(ref, ref, ag_send.at[1], agv_z.at[d, s], dz, 0)
                else:
                    ref = G.at[1, at(o, 0), :, halves[d]]
                    send(ref, ref, ag_send.at[1], agv_z.at[d, s], dz, 0)
                v_to_x(o)
            else:
                wait_for(G.at[1, at(o, 0), :, halves[d]], agv_z.at[d, s - 1])
        if s == H:
            v_to_x(H)
        for o in ((0,) if s == 1 else (1 - s, s - 1)):
            v_relay(o)
        for r in k_order:
            for d, dz in ((0, 1), (1, -1)):
                if s == H and r not in k_half[d]:
                    continue
                ref = G.at[0, at(-dz * s, r)]
                wait_for(ref, agk_z.at[d, s - 1, r])
                if s + 1 < H or (s + 1 == H and r in k_half[d]):
                    send(ref, ref, ag_send.at[0], agk_z.at[d, s, r], dz, 0)
    v_relay(H)

    loads[0].wait()
    loads[1].wait()
    def select(m, kv):
        table = G[kv].reshape(total, W)
        return jnp.dot(onehot[m], table, preferred_element_type=F32).astype(BF16)

    kb[...] = select(1, 0)
    for o in range(Z):
        v_relay_wait(o)
    vb[...] = select(1, 1)

    def softmax_t(k_h, q_h):
        st = lax.dot_general(k_h, q_h, NT, preferred_element_type=F32) * scale
        e = jnp.exp(st - jnp.max(st, axis=0, keepdims=True))
        return e / jnp.sum(e, axis=0, keepdims=True)

    for h in range(heads):
        cut = slice(h * HEAD, (h + 1) * HEAD)
        q_h, g_h = saved_v[:, cut], grad_v[:, cut]
        w = softmax_t(kb[:, cut], q_h)
        gw = lax.dot_general(vb[:, cut], g_h, NT, preferred_element_type=F32)
        centre = jnp.sum(w * gw, axis=0, keepdims=True)
        gst = (w * (gw - centre) * scale).astype(BF16)
        gs[h] = gst
        kt[:, cut] = jnp.dot(gst, q_h, preferred_element_type=F32).astype(BF16)
        vt[:, cut] = jnp.dot(w.astype(BF16), g_h, preferred_element_type=F32).astype(BF16)

    lane = lax.broadcasted_iota(jnp.int32, (1, picks * blk), 1)
    target = lane % blk
    for j in range(picks):
        target = target + jnp.where(lane // blk == j, places[1][j] * blk, 0)
    spread = lax.broadcasted_iota(jnp.int32, (total, picks * blk), 0) == target
    spread = jnp.where(spread, 1.0, 0.0).astype(BF16)
    for kv, terms in ((0, kt), (1, vt)):
        T[kv] = jnp.dot(spread, terms[...], preferred_element_type=F32).astype(BF16).reshape(
            Z * X, rows, W
        )

    def k_start(s):
        for r in k_order:
            for d, dz in ((0, 1), (1, -1)):
                if (s == 1 and r not in k_half[d]) or (s == 2 and r in k_half[d]):
                    continue
                if s > 2:
                    continue
                send(
                    T.at[0, at(dz * (H + 1 - s), r)], rkz.at[d, s - 1, r], rs_send.at[0],
                    rsk_z.at[d, s - 1, r], dz, 0,
                )

    def k_step(s):
        for r in k_order:
            for d, dz in ((0, 1), (1, -1)):
                if s == 2 and r not in k_half[d]:
                    continue
                mine = rkz.at[d, s - 2, r]
                wait_for(mine, rsk_z.at[d, s - 2, r])
                mine[...] = (
                    mine[...].astype(F32) + T[0, at(dz * (H + 1 - s), r)].astype(F32)
                ).astype(BF16)
                send(mine, rkz.at[d, s - 1, r], rs_send.at[0], rsk_z.at[d, s - 1, r], dz, 0)

    def v_a(o):
        for d, dx in ((0, 1), (1, -1)):
            send(
                T.at[1, at(o, 2), :, halves[d]], rva.at[d, o % Z], rs_send.at[1],
                rsv_a.at[d, o % Z], 0, dx,
            )

    def v_b(o):
        for d, dx in ((0, 1), (1, -1)):
            wait_for(rva.at[d, o % Z], rsv_a.at[d, o % Z])
            part = T.at[1, at(o, dx), :, halves[d]]
            part[...] = (part[...].astype(F32) + rva[d, o % Z].astype(F32)).astype(BF16)
            send(
                T.at[1, at(o, dx)], rvb.at[d, o % Z], rs_send.at[1], rsv_b.at[d, o % Z], 0, dx
            )

    def v_c(o):
        for d in range(2):
            wait_for(rvb.at[d, o % Z], rsv_b.at[d, o % Z])
        mine = T.at[1, at(o, 0)]
        mine[...] = (
            mine[...].astype(F32) + rvb[0, o % Z].astype(F32) + rvb[1, o % Z].astype(F32)
        ).astype(BF16)

    def v_z(s):
        for d, dz in ((0, 1), (1, -1)):
            o = dz * (H + 1 - s)
            if s == 1:
                send(
                    T.at[1, at(o, 0), :, halves[d]], rvz.at[d, 0, :, halves[d]], rs_send.at[1],
                    rsv_z.at[d, 0], dz, 0,
                )
                continue
            mine = T.at[1, at(o, 0)]
            if s == 2:
                got = rvz.at[d, 0, :, halves[d]]
                mine = T.at[1, at(o, 0), :, halves[d]]
            else:
                got = rvz.at[d, s - 2]
            wait_for(got, rsv_z.at[d, s - 2])
            mine[...] = (mine[...].astype(F32) + got[...].astype(F32)).astype(BF16)
            send(T.at[1, at(o, 0)], rvz.at[d, s - 1], rs_send.at[1], rsv_z.at[d, s - 1], dz, 0)

    def pair(i):
        return (i,) if i in (0, H) else (i, -i)

    def other_head(h):
        cut = slice(h * HEAD, (h + 1) * HEAD)

        @pl.when(pipe == 0)
        def _():
            s_h = stream_v[:, cut]
            w = softmax_t(kf[:, cut], s_h).astype(BF16)
            out = lax.dot_general(w, vf[:, cut], TN, preferred_element_type=F32)
            res[:, cut] = (s_h.astype(F32) + out).astype(BF16)

        @pl.when(pipe == 1)
        def _():
            out = lax.dot_general(gs[h], kb[:, cut], TN, preferred_element_type=F32)
            res[:, cut] = (grad_v[:, cut].astype(F32) + out).astype(BF16)

    def exchange(out_ref):
        return pltpu.make_async_remote_copy(
            src_ref=res, dst_ref=out_ref, send_sem=pipe_send, recv_sem=pipe_recv,
            device_id=(1 - pipe, dp, ten), device_id_type=pl.DeviceIdType.MESH,
        )

    def blank(out_ref):
        return pltpu.make_async_copy(zero, out_ref, zero_sem)

    k_start(1)
    for i in range(H, -1, -1):
        for o in pair(i):
            v_a(o)
        if i == H:
            k_start(2)
    zero[...] = jnp.zeros_like(zero)

    @pl.when(pipe == 0)
    def _():
        blank(next_ref).start()

    @pl.when(pipe == 1)
    def _():
        blank(back_ref).start()

    for o in pair(H) + pair(H - 1):
        v_b(o)
    loads[2].wait()

    @pl.when(pipe == 0)
    def _():
        kf[...] = select(0, 0)
        vf[...] = select(0, 1)

    done = 0
    for s in range(1, H + 1):
        if s >= 2:
            k_step(s)
        if H - 1 - s >= 0:
            for o in pair(H - 1 - s):
                v_b(o)
        for o in pair(H + 1 - s):
            v_c(o)
        v_z(s)
        if done < heads:
            other_head(done)
            done += 1
        if done == heads:
            done += 1

            @pl.when(pipe == 0)
            def _():
                exchange(next_ref).start()

            @pl.when(pipe == 1)
            def _():
                exchange(back_ref).start()

    last = []
    for r in k_order:
        mine = T.at[0, at(0, r)]
        total_r = mine[...].astype(F32)
        for d in range(2):
            got = rkz.at[d, H - 1, r]
            wait_for(got, rsk_z.at[d, H - 1, r])
            total_r = total_r + got[...].astype(F32)
        if r == 0:
            key_total = total_r
        else:
            mine[...] = total_r.astype(BF16)
            send(mine, rkx.at[r - 1], rs_send.at[0], rsk_x.at[r - 1], 0, r)
    v_c(0)
    value_total = T[1, dp].astype(F32)
    for d in range(2):
        got = rvz.at[d, H - 1]
        wait_for(got, rsv_z.at[d, H - 1])
        value_total = value_total + got[...].astype(F32)
    for i in range(2):
        vg_ref[i] = value_total[i * blk:(i + 1) * blk].astype(BF16)
    for r in (1, 3, 2):
        wait_for(rkx.at[r - 1], rsk_x.at[r - 1])
        key_total = key_total + rkx[r - 1].astype(F32)
    for i in range(2):
        kg_ref[i] = key_total[i * blk:(i + 1) * blk].astype(BF16)

    sent = Z * X - 1
    for kv in range(2):
        wait_for(G.at[kv, 0:sent], ag_send.at[kv])
        wait_for(T.at[kv, 0:sent], rs_send.at[kv])
    wait_for(res, pipe_send)
    wait_for(res, pipe_recv)
    wait_for(zero, zero_sem)


def local(stream_in, saved_in, grad_out, mem_keys, mem_values, owner_map, block_ids):
    Z = lax.axis_size("dp") // X
    H = Z // 2
    n_blk, blk = mem_keys.shape[1:3]
    picks = block_ids.shape[3]
    tokens, W = stream_in.shape[1:]
    heads = W // HEAD
    rows = n_blk * blk
    got = picks * blk
    DMA = pltpu.SemaphoreType.DMA
    anywhere = pl.BlockSpec(memory_space=pl.ANY)
    outs = pl.pallas_call(
        functools.partial(kernel, Z, blk, picks),
        out_shape=(
            jax.ShapeDtypeStruct((tokens, W), BF16),
            jax.ShapeDtypeStruct((tokens, W), BF16),
            jax.ShapeDtypeStruct((n_blk, blk, W), BF16),
            jax.ShapeDtypeStruct((n_blk, blk, W), BF16),
        ),
        in_specs=[anywhere] * 7,
        out_specs=(
            anywhere, anywhere,
            pl.BlockSpec(memory_space=pltpu.VMEM), pl.BlockSpec(memory_space=pltpu.VMEM),
        ),
        scratch_shapes=[
            pltpu.VMEM((tokens, W), BF16),
            pltpu.VMEM((tokens, W), BF16),
            pltpu.VMEM((tokens, W), BF16),
            pltpu.VMEM((2, n_blk, blk, W), BF16),
            pltpu.VMEM((2, Z * X, rows, W), BF16),
            pltpu.VMEM((2, Z * X, rows, W), BF16),
            pltpu.VMEM((2, got, Z * X * rows), BF16),
            pltpu.VMEM((got, W), BF16),
            pltpu.VMEM((got, W), BF16),
            pltpu.VMEM((got, W), BF16),
            pltpu.VMEM((got, W), BF16),
            pltpu.VMEM((got, W), BF16),
            pltpu.VMEM((got, W), BF16),
            pltpu.VMEM((heads, got, tokens), BF16),
            pltpu.VMEM((tokens, W), BF16),
            pltpu.VMEM((tokens, W), BF16),
            pltpu.VMEM((2, H, X, rows, W), BF16),
            pltpu.VMEM((2, H, rows, W), BF16),
            pltpu.VMEM((2, Z, rows, W // 2), BF16),
            pltpu.VMEM((2, Z, rows, W), BF16),
            pltpu.VMEM((X - 1, rows, W), BF16),
            pltpu.SMEM(owner_map.shape, jnp.int32),
            pltpu.SMEM(block_ids.shape, jnp.int32),
            DMA((3,)), DMA((4,)),
            DMA((X - 1,)), DMA((2, H, X)), DMA((2, H)), DMA((2, Z)), DMA((2, Z)), DMA((2,)),
            DMA((2, H, X)), DMA((X - 1,)), DMA((2, Z)), DMA((2, Z)), DMA((2, H)), DMA((2,)),
            DMA(()), DMA(()), DMA(()),
        ],
        compiler_params=pltpu.CompilerParams(
            collective_id=0, has_side_effects=True, vmem_limit_bytes=40 << 20
        ),
    )(
        stream_in[0], saved_in[0], grad_out[0], mem_keys[0], mem_values[0], owner_map, block_ids
    )
    return tuple(out[None] for out in outs)


def solution(mesh):
    in_specs = (
        P("pipe", "dp", "tensor"),
        P("pipe", "dp", "tensor"),
        P("pipe", "dp", "tensor"),
        P("pipe", "dp", None, "tensor"),
        P("pipe", "dp", None, "tensor"),
        P(),
        P(None, "pipe", "dp", None),
    )
    out_specs = (
        P("pipe", "dp", "tensor"),
        P("pipe", "dp", "tensor"),
        P("pipe", "dp", None, "tensor"),
        P("pipe", "dp", None, "tensor"),
    )
    return jax.shard_map(local, mesh=mesh, in_specs=in_specs, out_specs=out_specs, check_vma=False)
```

```python
import functools
import math

import jax
import jax.numpy as jnp
from jax import lax
from jax.experimental import pallas as pl
from jax.experimental.pallas import tpu as pltpu
from jax.sharding import PartitionSpec as P

HEAD = 128
X = 4
Z = 12
LANES = 128
BF16 = jnp.bfloat16
F32 = jnp.float32
NT = (((1,), (1,)), ((), ()))
TN = (((0,), (0,)), ((), ()))
MESH = pl.DeviceIdType.MESH
SIDES = ((0, 1), (1, -1))
FAR = (6, 5, -5, 4, -4)
VMEM_LIMIT = 60 << 20


def wait_for(ref, sem):
    pltpu.make_async_copy(ref, ref, sem).wait()


def main_kernel(
    blk, picks,
    stream_ref, saved_ref, grad_ref, mk_ref, mv_ref, om_ref, ids_ref,
    recv_ref, kg_ref, vg_ref,
    stream_v, saved_v, grad_v, mem_v, tab, G, S, C, pick, spread, kvb, kvf, terms, gs, res,
    T, rx, U, rr, rf, om_s, ids_s, tab_s,
    load_sem, small_sem, tab_send, tab_recv, tab_sem, agz, agx, agz_send, agx_send,
    rsx, rsr, rsf, rsx_send, rsz_send, pipe_send, pipe_recv,
):
    pipe, dp, ten = lax.axis_index("pipe"), lax.axis_index("dp"), lax.axis_index("tensor")
    z, x = dp // X, dp % X
    W = stream_v.shape[1]
    heads = W // HEAD
    keys = picks * blk
    both = 2 * blk
    total = Z * X * both
    scale = 1.0 / math.sqrt(HEAD)

    def zat(dz):
        return lax.rem(z + dz + Z, Z)

    def at(dz, dx):
        return zat(dz) * X + lax.rem(x + dx + X, X)

    def send(src, dst, ssem, rsem, dz, dx):
        pltpu.make_async_remote_copy(
            src_ref=src, dst_ref=dst, send_sem=ssem, recv_sem=rsem,
            device_id=(pipe, at(dz, dx), ten), device_id_type=MESH,
        ).start()

    mem_loads = [
        pltpu.make_async_copy(mk_ref, mem_v.at[0], small_sem.at[0]),
        pltpu.make_async_copy(mv_ref, mem_v.at[1], small_sem.at[1]),
    ]
    id_loads = [
        pltpu.make_async_copy(om_ref, om_s, small_sem.at[2]),
        pltpu.make_async_copy(ids_ref, ids_s, small_sem.at[3]),
    ]
    loads = [
        pltpu.make_async_copy(saved_ref, saved_v, load_sem.at[0]),
        pltpu.make_async_copy(grad_ref, grad_v, load_sem.at[1]),
        pltpu.make_async_copy(stream_ref, stream_v, load_sem.at[2]),
    ]
    for copy in mem_loads + id_loads:
        copy.start()
    barrier = pltpu.get_barrier_semaphore()
    partners = [(dz, 0) for dz in (3, -3, 2, -2, 1, -1)] + [(0, dx) for dx in range(1, X)]
    for dz, dx in partners:
        pl.semaphore_signal(
            barrier, inc=1, device_id=(pipe, at(dz, dx), ten), device_id_type=MESH
        )
    pl.semaphore_signal(barrier, inc=1, device_id=(1 - pipe, dp, ten), device_id_type=MESH)
    for copy in loads:
        copy.start()

    for copy in id_loads:
        copy.wait()
    places = [[om_s[ids_s[m, 0, 0, j]] for j in range(picks)] for m in range(2)]
    owners = [[place // 2 for place in row] for row in places]
    lane = lax.broadcasted_iota(jnp.int32, (8, LANES), 1)
    wanted = jnp.zeros((8, LANES), jnp.int32)
    for m in range(2):
        for j in range(picks):
            wanted = jnp.where(lane == owners[m][j], places[m][j] % 2, wanted)
    tab[0] = wanted
    for copy in mem_loads:
        copy.wait()
    for i in range(2):
        own = jnp.concatenate([mem_v[0, i].astype(F32), mem_v[1, i].astype(F32)], axis=0)
        G[z, i] = own.astype(BF16)
    pl.semaphore_wait(barrier, len(partners) + 1)

    for dz in (3, -3, 2, -2, 1, -1):
        send(G.at[z], G.at[z], agz_send, agz.at[(-dz) % Z], dz, 0)
    for dx in range(1, X):
        send(tab.at[0], tab.at[X - dx], tab_send, tab_recv.at[X - dx - 1], 0, dx)

    ramp = lax.broadcasted_iota(jnp.int32, (blk, total), 1) - lax.broadcasted_iota(
        jnp.int32, (blk, total), 0
    )
    for m in (1, 0):
        for kv in range(2):
            for j in range(0, picks, 2):
                pair = [
                    jnp.where(ramp == owners[m][i] * both + kv * blk, 1.0, 0.0).astype(F32)
                    for i in (j, j + 1)
                ]
                row = kv * keys + j * blk
                pick[m, row:row + both, :] = jnp.concatenate(pair, axis=0).astype(BF16)

    for dx in range(1, X):
        wait_for(tab.at[dx], tab_recv.at[dx - 1])
    to_scalars = pltpu.make_async_copy(tab, tab_s, tab_sem)
    to_scalars.start()
    for d, sg in SIDES:
        far = G.at[zat(-3 * sg)]
        wait_for(far, agz.at[(-3 * sg) % Z])
        send(far, far, agz_send, agz.at[(-4 * sg) % Z], sg, 0)
        send(far, far, agz_send, agz.at[(-5 * sg) % Z], 2 * sg, 0)
        part = G.at[zat(-3 * sg), d]
        send(part, part, agz_send, agz.at[6 + d * Z], 3 * sg, 0)
    to_scalars.wait()

    def slot(dx, o):
        return tab_s[dx, 0, at(o, 0)]

    for o in (0, 3, -3, 1, -1, 2, -2, 4, -4, 5, -5, 6):
        if o == 6:
            for d, _ in SIDES:
                wait_for(G.at[zat(6), d], agz.at[6 + d * Z])
        elif abs(o) not in (0, 3):
            wait_for(G.at[zat(o)], agz.at[o % Z])
        first, second = G[zat(o), 0], G[zat(o), 1]
        for dx in (2, 1, 3):
            S[dx - 1, o % Z] = jnp.where(slot(dx, o) == 1, second, first)
            send(
                S.at[dx - 1, o % Z], C.at[at(o, 0)], agx_send, agx.at[X - dx - 1, o % Z], 0, dx
            )
        C[at(o, 0)] = jnp.where(slot(0, o) == 1, second, first)

    column = lax.broadcasted_iota(jnp.int32, (1, 2 * keys), 1)
    target = column % blk + jnp.where(column >= keys, blk, 0)
    for j in range(picks):
        target = target + jnp.where((column % keys) // blk == j, owners[1][j] * both, 0)
    hits = lax.broadcasted_iota(jnp.int32, (total, 2 * keys), 0) == target
    spread[...] = jnp.where(hits, 1.0, 0.0).astype(BF16)

    for copy in loads:
        copy.wait()
    for o in (0, 3, -3, 1, -1, 2, -2, 4, -4, 5, -5, 6):
        for dx in range(1, X):
            wait_for(C.at[at(o, dx)], agx.at[dx - 1, o % Z])

    def select(m):
        return jnp.dot(
            pick[m], C[...].reshape(total, W), preferred_element_type=F32
        ).astype(BF16)

    def softmax_t(k_h, q_h):
        st = lax.dot_general(k_h, q_h, NT, preferred_element_type=F32) * scale
        e = jnp.exp(st - jnp.max(st, axis=0, keepdims=True))
        return e * (1.0 / jnp.sum(e, axis=0, keepdims=True))

    kvb[...] = select(1)
    for h in range(heads):
        cut = slice(h * HEAD, (h + 1) * HEAD)
        q_h, g_h = saved_v[:, cut], grad_v[:, cut]
        w = softmax_t(kvb[0:keys, cut], q_h)
        gw = lax.dot_general(kvb[keys:, cut], g_h, NT, preferred_element_type=F32)
        centre = jnp.sum(w * gw, axis=0, keepdims=True)
        gst = (w * (gw - centre) * scale).astype(BF16)
        gs[h] = gst
        terms[0:keys, cut] = jnp.dot(gst, q_h, preferred_element_type=F32).astype(BF16)
        terms[keys:, cut] = jnp.dot(
            w.astype(BF16), g_h, preferred_element_type=F32
        ).astype(BF16)
    T[...] = jnp.dot(spread[...], terms[...], preferred_element_type=F32).astype(BF16).reshape(
        Z * X, both, W
    )

    for o in FAR + (3, -3, 2, -2, 1, -1, 0):
        for dx in (2, 1, 3):
            send(T.at[at(o, dx)], rx.at[X - dx - 1, o % Z], rsx_send, rsx.at[X - dx - 1, o % Z], 0, dx)

    def exchange():
        return pltpu.make_async_remote_copy(
            src_ref=res, dst_ref=recv_ref, send_sem=pipe_send, recv_sem=pipe_recv,
            device_id=(1 - pipe, dp, ten), device_id_type=MESH,
        )

    @pl.when(pipe == 0)
    def _():
        kvf[...] = select(0)
        for h in range(heads):
            cut = slice(h * HEAD, (h + 1) * HEAD)
            s_h = stream_v[:, cut]
            w = softmax_t(kvf[0:keys, cut], s_h).astype(BF16)
            out = lax.dot_general(w, kvf[keys:, cut], TN, preferred_element_type=F32)
            res[:, cut] = (s_h.astype(F32) + out).astype(BF16)

    @pl.when(pipe == 1)
    def _():
        for h in range(heads):
            cut = slice(h * HEAD, (h + 1) * HEAD)
            out = lax.dot_general(gs[h], kvb[0:keys, cut], TN, preferred_element_type=F32)
            res[:, cut] = (grad_v[:, cut].astype(F32) + out).astype(BF16)

    exchange().start()

    def combine(o):
        for dx in range(1, X):
            wait_for(rx.at[dx - 1, o % Z], rsx.at[dx - 1, o % Z])
        sums = [None, None]
        for dx in range(X):
            part = (T[at(o, 0)] if dx == 0 else rx[dx - 1, o % Z]).astype(F32)
            second = slot(dx, o).astype(F32)
            for i, share in enumerate((1.0 - second, second)):
                sums[i] = part * share if sums[i] is None else sums[i] + part * share
        return sums

    def keep(o):
        for i, value in enumerate(combine(o)):
            U[o % Z, i] = value.astype(BF16)

    def relay(d, sg):
        mine = [U[(3 * sg) % Z, i].astype(F32) for i in range(2)]
        for k in range(2):
            wait_for(rr.at[d, k], rsr.at[d, k])
            mine = [mine[i] + rr[d, k, i].astype(F32) for i in range(2)]
        wait_for(rr.at[d, 2, d], rsr.at[d, 2])
        mine[d] = mine[d] + rr[d, 2, d].astype(F32)
        for i in range(2):
            U[(3 * sg) % Z, i] = mine[i].astype(BF16)
        send(U.at[(3 * sg) % Z], rf.at[d, 2], rsz_send, rsf.at[d, 2], 3 * sg, 0)

    keep(6)
    for d, sg in SIDES:
        send(U.at[6, d], rr.at[d, 2, d], rsz_send, rsr.at[d, 2], 3 * sg, 0)
    for k in (1, 0):
        for d, sg in SIDES:
            o = sg * (4 + k)
            keep(o)
            send(U.at[o % Z], rr.at[d, k], rsz_send, rsr.at[d, k], sg * (k + 1), 0)
    for d, sg in SIDES:
        keep(3 * sg)
    for d, sg in SIDES:
        keep(2 * sg)
        send(U.at[(2 * sg) % Z], rf.at[d, 1], rsz_send, rsf.at[d, 1], 2 * sg, 0)
    for d, sg in SIDES:
        relay(d, sg)
    for d, sg in SIDES:
        keep(sg)
        send(U.at[sg % Z], rf.at[d, 0], rsz_send, rsf.at[d, 0], sg, 0)
    last = combine(0)
    for k in range(3):
        for d, sg in SIDES:
            wait_for(rf.at[d, k], rsf.at[d, k])
            last = [last[i] + rf[d, k, i].astype(F32) for i in range(2)]
    for i in range(2):
        kg_ref[i] = last[i][0:blk].astype(BF16)
        vg_ref[i] = last[i][blk:].astype(BF16)

    wait_for(tab.at[0:X - 1], tab_send)
    wait_for(G.at[0:Z - 1], agz_send)
    wait_for(U.at[0:Z - 1], rsz_send)
    wait_for(C.at[0:(X - 1) * Z], agx_send)
    wait_for(T.at[0:(X - 1) * Z], rsx_send)
    wait_for(res, pipe_send)
    wait_for(res, pipe_recv)


def write_kernel(recv_ref, kg_ref, vg_ref, next_ref, back_ref, kgo_ref, vgo_ref, zero, sem):
    pipe = lax.axis_index("pipe")
    copies = [
        pltpu.make_async_copy(kg_ref, kgo_ref, sem.at[0]),
        pltpu.make_async_copy(vg_ref, vgo_ref, sem.at[1]),
    ]
    for copy in copies:
        copy.start()

    def finish(got_ref, blank_ref):
        got = pltpu.make_async_copy(recv_ref, got_ref, sem.at[2])
        got.start()
        zero[...] = jnp.zeros_like(zero)
        blank = pltpu.make_async_copy(zero, blank_ref, sem.at[3])
        blank.start()
        got.wait()
        blank.wait()

    @pl.when(pipe == 0)
    def _():
        finish(back_ref, next_ref)

    @pl.when(pipe == 1)
    def _():
        finish(next_ref, back_ref)

    for copy in copies:
        copy.wait()


def local(stream_in, saved_in, grad_out, mem_keys, mem_values, owner_map, block_ids):
    n_blk, blk = mem_keys.shape[1:3]
    picks = block_ids.shape[3]
    tokens, W = stream_in.shape[1:]
    heads = W // HEAD
    keys = picks * blk
    both = 2 * blk
    DMA = pltpu.SemaphoreType.DMA
    anywhere = pl.BlockSpec(memory_space=pl.ANY)
    in_vmem = pl.BlockSpec(memory_space=pltpu.VMEM)
    wide = jax.ShapeDtypeStruct((tokens, W), BF16)
    small = jax.ShapeDtypeStruct((n_blk, blk, W), BF16)
    recv, kg, vg = pl.pallas_call(
        functools.partial(main_kernel, blk, picks),
        out_shape=(wide, small, small),
        in_specs=[anywhere] * 7,
        out_specs=(anywhere, in_vmem, in_vmem),
        scratch_shapes=[
            pltpu.VMEM((tokens, W), BF16),
            pltpu.VMEM((tokens, W), BF16),
            pltpu.VMEM((tokens, W), BF16),
            pltpu.VMEM((2, n_blk, blk, W), BF16),
            pltpu.VMEM((X, 8, LANES), jnp.int32),
            pltpu.VMEM((Z, 2, both, W), BF16),
            pltpu.VMEM((X - 1, Z, both, W), BF16),
            pltpu.VMEM((Z * X, both, W), BF16),
            pltpu.VMEM((2, 2 * keys, Z * X * both), BF16),
            pltpu.VMEM((Z * X * both, 2 * keys), BF16),
            pltpu.VMEM((2 * keys, W), BF16),
            pltpu.VMEM((2 * keys, W), BF16),
            pltpu.VMEM((2 * keys, W), BF16),
            pltpu.VMEM((heads, keys, tokens), BF16),
            pltpu.VMEM((tokens, W), BF16),
            pltpu.VMEM((Z * X, both, W), BF16),
            pltpu.VMEM((X - 1, Z, both, W), BF16),
            pltpu.VMEM((Z, 2, both, W), BF16),
            pltpu.VMEM((2, 3, 2, both, W), BF16),
            pltpu.VMEM((2, 3, 2, both, W), BF16),
            pltpu.SMEM(owner_map.shape, jnp.int32),
            pltpu.SMEM(block_ids.shape, jnp.int32),
            pltpu.SMEM((X, 8, LANES), jnp.int32),
            DMA((3,)), DMA((4,)), DMA(()), DMA((X - 1,)), DMA(()),
            DMA((2 * Z,)), DMA((X - 1, Z)), DMA(()), DMA(()),
            DMA((X - 1, Z)), DMA((2, 3)), DMA((2, 3)), DMA(()), DMA(()), DMA(()), DMA(()),
        ],
        compiler_params=pltpu.CompilerParams(
            collective_id=0, has_side_effects=True, vmem_limit_bytes=VMEM_LIMIT
        ),
    )(
        stream_in[0], saved_in[0], grad_out[0], mem_keys[0], mem_values[0], owner_map, block_ids
    )
    outs = pl.pallas_call(
        write_kernel,
        out_shape=(wide, wide, small, small),
        in_specs=[anywhere] * 3,
        out_specs=(anywhere,) * 4,
        scratch_shapes=[pltpu.VMEM((tokens, W), BF16), DMA((4,))],
        compiler_params=pltpu.CompilerParams(vmem_limit_bytes=VMEM_LIMIT),
    )(recv, kg, vg)
    return tuple(out[None] for out in outs)


def solution(mesh):
    in_specs = (
        P("pipe", "dp", "tensor"),
        P("pipe", "dp", "tensor"),
        P("pipe", "dp", "tensor"),
        P("pipe", "dp", None, "tensor"),
        P("pipe", "dp", None, "tensor"),
        P(),
        P(None, "pipe", "dp", None),
    )
    out_specs = (
        P("pipe", "dp", "tensor"),
        P("pipe", "dp", "tensor"),
        P("pipe", "dp", None, "tensor"),
        P("pipe", "dp", None, "tensor"),
    )
    return jax.shard_map(local, mesh=mesh, in_specs=in_specs, out_specs=out_specs, check_vma=False)
```

```python
import functools
import math

import jax
import jax.numpy as jnp
from jax import lax
from jax.experimental import pallas as pl
from jax.experimental.pallas import tpu as pltpu
from jax.sharding import PartitionSpec as P

HEAD = 128
X = 4
Z = 12
LANES = 128
BF16 = jnp.bfloat16
F32 = jnp.float32
NT = (((1,), (1,)), ((), ()))
TN = (((0,), (0,)), ((), ()))
MESH = pl.DeviceIdType.MESH
SIDES = ((0, 1), (1, -1))
FAR = (6, 5, -5, 4, -4)
VMEM_LIMIT = 40 << 20


def wait_for(ref, sem):
    pltpu.make_async_copy(ref, ref, sem).wait()


def main_kernel(
    blk, picks,
    stream_ref, saved_ref, grad_ref, mk_ref, mv_ref, om_ref, ids_ref,
    recv_ref, kg_ref, vg_ref,
    stream_v, saved_v, grad_v, mem_v, tab, G, S, C, pick, spread, kvb, kvf, terms, gs, res,
    T, rx, U, rr, rf, om_s, ids_s, tab_s,
    load_sem, small_sem, tab_send, tab_recv, tab_sem, agz, agx, agz_send, agx_send,
    rsx, rsr, rsf, rsx_send, rsz_send, pipe_send, pipe_recv,
):
    pipe, dp, ten = lax.axis_index("pipe"), lax.axis_index("dp"), lax.axis_index("tensor")
    z, x = dp // X, dp % X
    W = stream_v.shape[1]
    heads = W // HEAD
    keys = picks * blk
    both = 2 * blk
    total = Z * X * both
    scale = 1.0 / math.sqrt(HEAD)

    def zat(dz):
        return lax.rem(z + dz + Z, Z)

    def at(dz, dx):
        return zat(dz) * X + lax.rem(x + dx + X, X)

    def send(src, dst, ssem, rsem, dz, dx):
        pltpu.make_async_remote_copy(
            src_ref=src, dst_ref=dst, send_sem=ssem, recv_sem=rsem,
            device_id=(pipe, at(dz, dx), ten), device_id_type=MESH,
        ).start()

    mem_loads = [
        pltpu.make_async_copy(mk_ref, mem_v.at[0], small_sem.at[0]),
        pltpu.make_async_copy(mv_ref, mem_v.at[1], small_sem.at[1]),
    ]
    id_loads = [
        pltpu.make_async_copy(om_ref, om_s, small_sem.at[2]),
        pltpu.make_async_copy(ids_ref, ids_s, small_sem.at[3]),
    ]
    loads = [
        pltpu.make_async_copy(saved_ref, saved_v, load_sem.at[0]),
        pltpu.make_async_copy(grad_ref, grad_v, load_sem.at[1]),
        pltpu.make_async_copy(stream_ref, stream_v, load_sem.at[2]),
    ]
    for copy in mem_loads + id_loads:
        copy.start()
    barrier = pltpu.get_barrier_semaphore()
    partners = [(dz, 0) for dz in (3, -3, 2, -2, 1, -1)] + [(0, dx) for dx in range(1, X)]
    for dz, dx in partners:
        pl.semaphore_signal(
            barrier, inc=1, device_id=(pipe, at(dz, dx), ten), device_id_type=MESH
        )
    pl.semaphore_signal(barrier, inc=1, device_id=(1 - pipe, dp, ten), device_id_type=MESH)
    for copy in loads:
        copy.start()

    for copy in id_loads:
        copy.wait()
    places = [[om_s[ids_s[m, 0, 0, j]] for j in range(picks)] for m in range(2)]
    owners = [[place // 2 for place in row] for row in places]
    lane = lax.broadcasted_iota(jnp.int32, (8, LANES), 1)
    wanted = jnp.zeros((8, LANES), jnp.int32)
    for m in range(2):
        for j in range(picks):
            wanted = jnp.where(lane == owners[m][j], places[m][j] % 2, wanted)
    tab[0] = wanted
    for copy in mem_loads:
        copy.wait()
    for i in range(2):
        own = jnp.concatenate([mem_v[0, i].astype(F32), mem_v[1, i].astype(F32)], axis=0)
        G[z, i] = own.astype(BF16)
    pl.semaphore_wait(barrier, len(partners) + 1)

    for dz in (3, -3, 2, -2, 1, -1):
        send(G.at[z], G.at[z], agz_send, agz.at[(-dz) % Z], dz, 0)
    for dx in range(1, X):
        send(tab.at[0], tab.at[X - dx], tab_send, tab_recv.at[X - dx - 1], 0, dx)

    ramp = lax.broadcasted_iota(jnp.int32, (blk, total), 1) - lax.broadcasted_iota(
        jnp.int32, (blk, total), 0
    )
    for m in (1, 0):
        for kv in range(2):
            for j in range(0, picks, 2):
                pair = [
                    jnp.where(ramp == owners[m][i] * both + kv * blk, 1.0, 0.0).astype(F32)
                    for i in (j, j + 1)
                ]
                row = kv * keys + j * blk
                pick[m, row:row + both, :] = jnp.concatenate(pair, axis=0).astype(BF16)

    for dx in range(1, X):
        wait_for(tab.at[dx], tab_recv.at[dx - 1])
    to_scalars = pltpu.make_async_copy(tab, tab_s, tab_sem)
    to_scalars.start()
    for d, sg in SIDES:
        far = G.at[zat(-3 * sg)]
        wait_for(far, agz.at[(-3 * sg) % Z])
        send(far, far, agz_send, agz.at[(-4 * sg) % Z], sg, 0)
        send(far, far, agz_send, agz.at[(-5 * sg) % Z], 2 * sg, 0)
        part = G.at[zat(-3 * sg), d]
        send(part, part, agz_send, agz.at[6 + d * Z], 3 * sg, 0)
    to_scalars.wait()

    def slot(dx, o):
        return tab_s[dx, 0, at(o, 0)]

    for o in (0, 3, -3, 1, -1, 2, -2, 4, -4, 5, -5, 6):
        if o == 6:
            for d, _ in SIDES:
                wait_for(G.at[zat(6), d], agz.at[6 + d * Z])
        elif abs(o) not in (0, 3):
            wait_for(G.at[zat(o)], agz.at[o % Z])
        first, second = G[zat(o), 0], G[zat(o), 1]
        for dx in (2, 1, 3):
            S[dx - 1, o % Z] = jnp.where(slot(dx, o) == 1, second, first)
            send(
                S.at[dx - 1, o % Z], C.at[at(o, 0)], agx_send, agx.at[X - dx - 1, o % Z], 0, dx
            )
        C[at(o, 0)] = jnp.where(slot(0, o) == 1, second, first)

    column = lax.broadcasted_iota(jnp.int32, (1, 2 * keys), 1)
    target = column % blk + jnp.where(column >= keys, blk, 0)
    for j in range(picks):
        target = target + jnp.where((column % keys) // blk == j, owners[1][j] * both, 0)
    hits = lax.broadcasted_iota(jnp.int32, (total, 2 * keys), 0) == target
    spread[...] = jnp.where(hits, 1.0, 0.0).astype(BF16)

    for copy in loads:
        copy.wait()
    for o in (0, 3, -3, 1, -1, 2, -2, 4, -4, 5, -5, 6):
        for dx in range(1, X):
            wait_for(C.at[at(o, dx)], agx.at[dx - 1, o % Z])

    def select(m):
        return jnp.dot(
            pick[m], C[...].reshape(total, W), preferred_element_type=F32
        ).astype(BF16)

    def softmax_t(k_h, q_h):
        st = lax.dot_general(k_h, q_h, NT, preferred_element_type=F32) * scale
        e = jnp.exp(st - jnp.max(st, axis=0, keepdims=True))
        return e * (1.0 / jnp.sum(e, axis=0, keepdims=True))

    kvb[...] = select(1)
    for h in range(heads):
        cut = slice(h * HEAD, (h + 1) * HEAD)
        q_h, g_h = saved_v[:, cut], grad_v[:, cut]
        w = softmax_t(kvb[0:keys, cut], q_h)
        gw = lax.dot_general(kvb[keys:, cut], g_h, NT, preferred_element_type=F32)
        centre = jnp.sum(w * gw, axis=0, keepdims=True)
        gst = (w * (gw - centre) * scale).astype(BF16)
        gs[h] = gst
        terms[0:keys, cut] = jnp.dot(gst, q_h, preferred_element_type=F32).astype(BF16)
        terms[keys:, cut] = jnp.dot(
            w.astype(BF16), g_h, preferred_element_type=F32
        ).astype(BF16)
    T[...] = jnp.dot(spread[...], terms[...], preferred_element_type=F32).astype(BF16).reshape(
        Z * X, both, W
    )

    for o in FAR + (3, -3, 2, -2, 1, -1, 0):
        for dx in (2, 1, 3):
            send(T.at[at(o, dx)], rx.at[X - dx - 1, o % Z], rsx_send, rsx.at[X - dx - 1, o % Z], 0, dx)

    def exchange():
        return pltpu.make_async_remote_copy(
            src_ref=res, dst_ref=recv_ref, send_sem=pipe_send, recv_sem=pipe_recv,
            device_id=(1 - pipe, dp, ten), device_id_type=MESH,
        )

    @pl.when(pipe == 0)
    def _():
        kvf[...] = select(0)
        for h in range(heads):
            cut = slice(h * HEAD, (h + 1) * HEAD)
            s_h = stream_v[:, cut]
            w = softmax_t(kvf[0:keys, cut], s_h).astype(BF16)
            out = lax.dot_general(w, kvf[keys:, cut], TN, preferred_element_type=F32)
            res[:, cut] = (s_h.astype(F32) + out).astype(BF16)

    @pl.when(pipe == 1)
    def _():
        for h in range(heads):
            cut = slice(h * HEAD, (h + 1) * HEAD)
            out = lax.dot_general(gs[h], kvb[0:keys, cut], TN, preferred_element_type=F32)
            res[:, cut] = (grad_v[:, cut].astype(F32) + out).astype(BF16)

    exchange().start()

    def combine(o):
        for dx in range(1, X):
            wait_for(rx.at[dx - 1, o % Z], rsx.at[dx - 1, o % Z])
        sums = [None, None]
        for dx in range(X):
            part = (T[at(o, 0)] if dx == 0 else rx[dx - 1, o % Z]).astype(F32)
            second = slot(dx, o).astype(F32)
            for i, share in enumerate((1.0 - second, second)):
                sums[i] = part * share if sums[i] is None else sums[i] + part * share
        return sums

    def keep(o):
        for i, value in enumerate(combine(o)):
            U[o % Z, i] = value.astype(BF16)

    def relay(d, sg):
        mine = [U[(3 * sg) % Z, i].astype(F32) for i in range(2)]
        for k in range(2):
            wait_for(rr.at[d, k], rsr.at[d, k])
            mine = [mine[i] + rr[d, k, i].astype(F32) for i in range(2)]
        wait_for(rr.at[d, 2, d], rsr.at[d, 2])
        mine[d] = mine[d] + rr[d, 2, d].astype(F32)
        for i in range(2):
            U[(3 * sg) % Z, i] = mine[i].astype(BF16)
        send(U.at[(3 * sg) % Z], rf.at[d, 2], rsz_send, rsf.at[d, 2], 3 * sg, 0)

    keep(6)
    for d, sg in SIDES:
        send(U.at[6, d], rr.at[d, 2, d], rsz_send, rsr.at[d, 2], 3 * sg, 0)
    for k in (1, 0):
        for d, sg in SIDES:
            o = sg * (4 + k)
            keep(o)
            send(U.at[o % Z], rr.at[d, k], rsz_send, rsr.at[d, k], sg * (k + 1), 0)
    for d, sg in SIDES:
        keep(3 * sg)
    for d, sg in SIDES:
        keep(2 * sg)
        send(U.at[(2 * sg) % Z], rf.at[d, 1], rsz_send, rsf.at[d, 1], 2 * sg, 0)
    for d, sg in SIDES:
        relay(d, sg)
    for d, sg in SIDES:
        keep(sg)
        send(U.at[sg % Z], rf.at[d, 0], rsz_send, rsf.at[d, 0], sg, 0)
    last = combine(0)
    for k in range(3):
        for d, sg in SIDES:
            wait_for(rf.at[d, k], rsf.at[d, k])
            last = [last[i] + rf[d, k, i].astype(F32) for i in range(2)]
    for i in range(2):
        kg_ref[i] = last[i][0:blk].astype(BF16)
        vg_ref[i] = last[i][blk:].astype(BF16)

    wait_for(tab.at[0:X - 1], tab_send)
    wait_for(G.at[0:Z - 1], agz_send)
    wait_for(U.at[0:Z - 1], rsz_send)
    wait_for(C.at[0:(X - 1) * Z], agx_send)
    wait_for(T.at[0:(X - 1) * Z], rsx_send)
    wait_for(res, pipe_send)
    wait_for(res, pipe_recv)


def write_kernel(recv_ref, kg_ref, vg_ref, next_ref, back_ref, kgo_ref, vgo_ref, zero, sem):
    pipe = lax.axis_index("pipe")
    copies = [
        pltpu.make_async_copy(kg_ref, kgo_ref, sem.at[0]),
        pltpu.make_async_copy(vg_ref, vgo_ref, sem.at[1]),
    ]
    for copy in copies:
        copy.start()

    def finish(got_ref, blank_ref):
        got = pltpu.make_async_copy(recv_ref, got_ref, sem.at[2])
        got.start()
        zero[...] = jnp.zeros_like(zero)
        blank = pltpu.make_async_copy(zero, blank_ref, sem.at[3])
        blank.start()
        got.wait()
        blank.wait()

    @pl.when(pipe == 0)
    def _():
        finish(back_ref, next_ref)

    @pl.when(pipe == 1)
    def _():
        finish(next_ref, back_ref)

    for copy in copies:
        copy.wait()


def local(stream_in, saved_in, grad_out, mem_keys, mem_values, owner_map, block_ids):
    n_blk, blk = mem_keys.shape[1:3]
    picks = block_ids.shape[3]
    tokens, W = stream_in.shape[1:]
    heads = W // HEAD
    keys = picks * blk
    both = 2 * blk
    DMA = pltpu.SemaphoreType.DMA
    anywhere = pl.BlockSpec(memory_space=pl.ANY)
    in_vmem = pl.BlockSpec(memory_space=pltpu.VMEM)
    wide = jax.ShapeDtypeStruct((tokens, W), BF16)
    small = jax.ShapeDtypeStruct((n_blk, blk, W), BF16)
    held = pltpu.VMEM((tokens, W), BF16)
    held_small = pltpu.VMEM((n_blk, blk, W), BF16)
    operands = (
        stream_in[0], saved_in[0], grad_out[0], mem_keys[0], mem_values[0], owner_map, block_ids
    )
    recv, kg, vg = pl.pallas_call(
        functools.partial(main_kernel, blk, picks),
        out_shape=(held, held_small, held_small),
        in_specs=[anywhere] * 7,
        out_specs=(anywhere, in_vmem, in_vmem),
        scratch_shapes=[
            pltpu.VMEM((tokens, W), BF16),
            pltpu.VMEM((tokens, W), BF16),
            pltpu.VMEM((tokens, W), BF16),
            pltpu.VMEM((2, n_blk, blk, W), BF16),
            pltpu.VMEM((X, 8, LANES), jnp.int32),
            pltpu.VMEM((Z, 2, both, W), BF16),
            pltpu.VMEM((X - 1, Z, both, W), BF16),
            pltpu.VMEM((Z * X, both, W), BF16),
            pltpu.VMEM((2, 2 * keys, Z * X * both), BF16),
            pltpu.VMEM((Z * X * both, 2 * keys), BF16),
            pltpu.VMEM((2 * keys, W), BF16),
            pltpu.VMEM((2 * keys, W), BF16),
            pltpu.VMEM((2 * keys, W), BF16),
            pltpu.VMEM((heads, keys, tokens), BF16),
            pltpu.VMEM((tokens, W), BF16),
            pltpu.VMEM((Z * X, both, W), BF16),
            pltpu.VMEM((X - 1, Z, both, W), BF16),
            pltpu.VMEM((Z, 2, both, W), BF16),
            pltpu.VMEM((2, 3, 2, both, W), BF16),
            pltpu.VMEM((2, 3, 2, both, W), BF16),
            pltpu.SMEM(owner_map.shape, jnp.int32),
            pltpu.SMEM(block_ids.shape, jnp.int32),
            pltpu.SMEM((X, 8, LANES), jnp.int32),
            DMA((3,)), DMA((4,)), DMA(()), DMA((X - 1,)), DMA(()),
            DMA((2 * Z,)), DMA((X - 1, Z)), DMA(()), DMA(()),
            DMA((X - 1, Z)), DMA((2, 3)), DMA((2, 3)), DMA(()), DMA(()), DMA(()), DMA(()),
        ],
        compiler_params=pltpu.CompilerParams(
            collective_id=0, has_side_effects=True, vmem_limit_bytes=VMEM_LIMIT
        ),
    )(
        *(pltpu.with_memory_space_constraint(operand, pltpu.HBM) for operand in operands)
    )
    outs = pl.pallas_call(
        write_kernel,
        out_shape=(wide, wide, small, small),
        in_specs=[anywhere] * 3,
        out_specs=(anywhere,) * 4,
        scratch_shapes=[pltpu.VMEM((tokens, W), BF16), DMA((4,))],
        compiler_params=pltpu.CompilerParams(vmem_limit_bytes=VMEM_LIMIT),
    )(recv, kg, vg)
    return tuple(out[None] for out in outs)


def solution(mesh):
    in_specs = (
        P("pipe", "dp", "tensor"),
        P("pipe", "dp", "tensor"),
        P("pipe", "dp", "tensor"),
        P("pipe", "dp", None, "tensor"),
        P("pipe", "dp", None, "tensor"),
        P(),
        P(None, "pipe", "dp", None),
    )
    out_specs = (
        P("pipe", "dp", "tensor"),
        P("pipe", "dp", "tensor"),
        P("pipe", "dp", None, "tensor"),
        P("pipe", "dp", None, "tensor"),
    )
    return jax.shard_map(local, mesh=mesh, in_specs=in_specs, out_specs=out_specs, check_vma=False)
```

```python
import functools
import math

import jax
import jax.numpy as jnp
from jax import lax
from jax.experimental import pallas as pl
from jax.experimental.pallas import tpu as pltpu
from jax.sharding import PartitionSpec as P

HEAD = 128
X = 4
Z = 12
LANES = 128
BF16 = jnp.bfloat16
F32 = jnp.float32
NT = (((1,), (1,)), ((), ()))
TN = (((0,), (0,)), ((), ()))
MESH = pl.DeviceIdType.MESH
SIDES = ((0, 1), (1, -1))
FAR = (6, 5, -5, 4, -4)
VMEM_LIMIT = 40 << 20


def wait_for(ref, sem):
    pltpu.make_async_copy(ref, ref, sem).wait()


def main_kernel(
    blk, picks,
    stream_ref, saved_ref, grad_ref, mk_ref, mv_ref, om_ref, ids_ref,
    recv_ref, kg_ref, vg_ref,
    stream_v, saved_v, grad_v, saved_t, grad_t, mem_v, tab, G, D, S, C, pick, spread, kvb, kvf, terms, gs, res,
    T, rx, U, rr, rf, om_s, ids_s, tab_s,
    load_sem, small_sem, tab_send, tab_recv, tab_sem, agz, agd, agx, agz_send, agx_send,
    rsx, rsr, rsf, rsx_send, rsz_send, pipe_send, pipe_recv,
):
    pipe, dp, ten = lax.axis_index("pipe"), lax.axis_index("dp"), lax.axis_index("tensor")
    z, x = dp // X, dp % X
    W = stream_v.shape[1]
    heads = W // HEAD
    keys = picks * blk
    both = 2 * blk
    total = Z * X * both
    scale = 1.0 / math.sqrt(HEAD)

    def zat(dz):
        return lax.rem(z + dz + Z, Z)

    def at(dz, dx):
        return zat(dz) * X + lax.rem(x + dx + X, X)

    def send(src, dst, ssem, rsem, dz, dx):
        pltpu.make_async_remote_copy(
            src_ref=src, dst_ref=dst, send_sem=ssem, recv_sem=rsem,
            device_id=(pipe, at(dz, dx), ten), device_id_type=MESH,
        ).start()

    mem_loads = [
        pltpu.make_async_copy(mk_ref, mem_v.at[0], small_sem.at[0]),
        pltpu.make_async_copy(mv_ref, mem_v.at[1], small_sem.at[1]),
    ]
    id_loads = [
        pltpu.make_async_copy(om_ref, om_s, small_sem.at[2]),
        pltpu.make_async_copy(ids_ref, ids_s, small_sem.at[3]),
    ]
    loads = [
        pltpu.make_async_copy(saved_ref, saved_v, load_sem.at[0]),
        pltpu.make_async_copy(grad_ref, grad_v, load_sem.at[1]),
        pltpu.make_async_copy(stream_ref, stream_v, load_sem.at[2]),
    ]
    for copy in mem_loads + id_loads:
        copy.start()
    barrier = pltpu.get_barrier_semaphore()
    partners = [(dz, 0) for dz in (3, -3, 2, -2, 1, -1)] + [(0, dx) for dx in range(1, X)]
    for dz, dx in partners:
        pl.semaphore_signal(
            barrier, inc=1, device_id=(pipe, at(dz, dx), ten), device_id_type=MESH
        )
    pl.semaphore_signal(barrier, inc=1, device_id=(1 - pipe, dp, ten), device_id_type=MESH)
    for copy in loads:
        copy.start()

    for copy in mem_loads:
        copy.wait()
    for i in range(2):
        own = jnp.concatenate([mem_v[0, i].astype(F32), mem_v[1, i].astype(F32)], axis=0)
        G[z, i] = own.astype(BF16)

    for copy in id_loads:
        copy.wait()
    places = [[om_s[ids_s[m, 0, 0, j]] for j in range(picks)] for m in range(2)]
    owners = [[place // 2 for place in row] for row in places]
    lane = lax.broadcasted_iota(jnp.int32, (8, LANES), 1)
    wanted = jnp.zeros((8, LANES), jnp.int32)
    for m in range(2):
        for j in range(picks):
            wanted = jnp.where(lane == owners[m][j], places[m][j] % 2, wanted)
    tab[0] = wanted
    pl.semaphore_wait(barrier, len(partners) + 1)

    for dx in range(1, X):
        send(tab.at[0], tab.at[X - dx], tab_send, tab_recv.at[X - dx - 1], 0, dx)
    for dz in (1, -1, 3, -3, 2, -2):
        send(G.at[z], G.at[z], agz_send, agz.at[(-dz) % Z], dz, 0)
    for dx in (2, 1, 3):
        send(G.at[z], D.at[X - dx - 1], agx_send, agd.at[X - dx - 1], 0, dx)

    ramp = lax.broadcasted_iota(jnp.int32, (blk, total), 1) - lax.broadcasted_iota(
        jnp.int32, (blk, total), 0
    )
    for m in (1, 0):
        for kv in range(2):
            for j in range(0, picks, 2):
                pair = [
                    jnp.where(ramp == owners[m][i] * both + kv * blk, 1.0, 0.0).astype(F32)
                    for i in (j, j + 1)
                ]
                row = kv * keys + j * blk
                pick[m, row:row + both, :] = jnp.concatenate(pair, axis=0).astype(BF16)

    for dx in range(1, X):
        wait_for(tab.at[dx], tab_recv.at[dx - 1])
    to_scalars = pltpu.make_async_copy(tab, tab_s, tab_sem)
    to_scalars.start()
    to_scalars.wait()

    def slot(dx, o):
        return tab_s[dx, 0, at(o, 0)]

    def to_peers(o):
        if o == 6:
            for d, _ in SIDES:
                wait_for(G.at[zat(6), d], agz.at[6 + d * Z])
        elif abs(o) != 3:
            wait_for(G.at[zat(o)], agz.at[o % Z])
        first, second = G[zat(o), 0], G[zat(o), 1]
        for dx in (2, 1, 3):
            S[dx - 1, o % Z] = jnp.where(slot(dx, o) == 1, second, first)
            send(
                S.at[dx - 1, o % Z], C.at[at(o, 0)], agx_send, agx.at[X - dx - 1, o % Z], 0, dx
            )
        C[at(o, 0)] = jnp.where(slot(0, o) == 1, second, first)

    to_peers(1)
    to_peers(-1)
    for d, sg in SIDES:
        far = G.at[zat(-3 * sg)]
        wait_for(far, agz.at[(-3 * sg) % Z])
        send(far, far, agz_send, agz.at[(-4 * sg) % Z], sg, 0)
        send(far, far, agz_send, agz.at[(-5 * sg) % Z], 2 * sg, 0)
        part = G.at[zat(-3 * sg), d]
        send(part, part, agz_send, agz.at[6 + d * Z], 3 * sg, 0)
    for o in (3, -3, 2, -2):
        to_peers(o)
    C[dp] = jnp.where(slot(0, 0) == 1, G[z, 1], G[z, 0])
    for dx in range(1, X):
        wait_for(D.at[dx - 1], agd.at[dx - 1])
        mine = tab_s[0, 0, at(0, dx)]
        C[at(0, dx)] = jnp.where(mine == 1, D[dx - 1, 1], D[dx - 1, 0])
    for copy in loads:
        copy.wait()
    for h in range(heads // 2):
        cut = slice(h * HEAD, (h + 1) * HEAD)
        saved_t[h], grad_t[h] = saved_v[:, cut].T, grad_v[:, cut].T
    for o in (4, -4, 5, -5, 6):
        to_peers(o)
    for h in range(heads // 2, heads):
        cut = slice(h * HEAD, (h + 1) * HEAD)
        saved_t[h], grad_t[h] = saved_v[:, cut].T, grad_v[:, cut].T

    column = lax.broadcasted_iota(jnp.int32, (1, 2 * keys), 1)
    target = column % blk + jnp.where(column >= keys, blk, 0)
    for j in range(picks):
        target = target + jnp.where((column % keys) // blk == j, owners[1][j] * both, 0)
    hits = lax.broadcasted_iota(jnp.int32, (total, 2 * keys), 0) == target
    spread[...] = jnp.where(hits, 1.0, 0.0).astype(BF16)

    for o in (1, -1, 3, -3, 2, -2, 4, -4, 5, -5, 6):
        for dx in range(1, X):
            wait_for(C.at[at(o, dx)], agx.at[dx - 1, o % Z])

    def select(m):
        return jnp.dot(
            pick[m], C[...].reshape(total, W), preferred_element_type=F32
        ).astype(BF16)

    def powers(st):
        return jnp.exp2((st - jnp.max(st, axis=0, keepdims=True)) * (scale * math.log2(math.e)))

    def backward_head(h):
        cut = slice(h * HEAD, (h + 1) * HEAD)
        e = powers(jnp.dot(kvb[0:keys, cut], saved_t[h], preferred_element_type=F32))
        gw = jnp.dot(kvb[keys:, cut], grad_t[h], preferred_element_type=F32)
        share = 1.0 / jnp.sum(e, axis=0, keepdims=True)
        centre = jnp.sum(e * gw, axis=0, keepdims=True) * share
        gst = (e * (share * scale) * (gw - centre)).astype(BF16)
        gs[h] = gst
        terms[0:keys, cut] = jnp.dot(
            gst, saved_v[:, cut], preferred_element_type=F32
        ).astype(BF16)
        terms[keys:, cut] = jnp.dot(
            (e * share).astype(BF16), grad_v[:, cut], preferred_element_type=F32
        ).astype(BF16)

    def to_column(o, part):
        index = o % Z if part is None else o % Z + part * Z
        cols = slice(0, W) if part is None else slice(part * W // 2, (part + 1) * W // 2)
        for dx in (2, 1, 3):
            send(
                T.at[at(o, dx), :, cols], rx.at[X - dx - 1, o % Z, :, cols],
                rsx_send, rsx.at[X - dx - 1, index], 0, dx,
            )

    kvb[...] = select(1)
    for part in range(2):
        for h in range(part * heads // 2, (part + 1) * heads // 2):
            backward_head(h)
        cols = slice(part * W // 2, (part + 1) * W // 2)
        T[:, :, cols] = jnp.dot(
            spread[...], terms[:, cols], preferred_element_type=F32
        ).astype(BF16).reshape(Z * X, both, W // 2)
        for o in FAR:
            to_column(o, part)
    for o in (3, -3, 2, -2, 1, -1, 0):
        to_column(o, None)

    def exchange():
        return pltpu.make_async_remote_copy(
            src_ref=res, dst_ref=recv_ref, send_sem=pipe_send, recv_sem=pipe_recv,
            device_id=(1 - pipe, dp, ten), device_id_type=MESH,
        )

    @pl.when(pipe == 0)
    def _():
        kvf[...] = select(0)
        for h in range(heads):
            cut = slice(h * HEAD, (h + 1) * HEAD)
            s_h = stream_v[:, cut]
            e = powers(lax.dot_general(kvf[0:keys, cut], s_h, NT, preferred_element_type=F32))
            w = (e * (1.0 / jnp.sum(e, axis=0, keepdims=True))).astype(BF16)
            out = lax.dot_general(w, kvf[keys:, cut], TN, preferred_element_type=F32)
            res[:, cut] = (s_h.astype(F32) + out).astype(BF16)

    @pl.when(pipe == 1)
    def _():
        for h in range(heads):
            cut = slice(h * HEAD, (h + 1) * HEAD)
            out = lax.dot_general(gs[h], kvb[0:keys, cut], TN, preferred_element_type=F32)
            res[:, cut] = (grad_v[:, cut].astype(F32) + out).astype(BF16)

    exchange().start()

    def combine(o):
        for dx in range(1, X):
            if o in FAR:
                for part in range(2):
                    cols = slice(part * W // 2, (part + 1) * W // 2)
                    wait_for(rx.at[dx - 1, o % Z, :, cols], rsx.at[dx - 1, o % Z + part * Z])
            else:
                wait_for(rx.at[dx - 1, o % Z], rsx.at[dx - 1, o % Z])
        sums = [None, None]
        for dx in range(X):
            part = (T[at(o, 0)] if dx == 0 else rx[dx - 1, o % Z]).astype(F32)
            second = slot(dx, o).astype(F32)
            for i, share in enumerate((1.0 - second, second)):
                sums[i] = part * share if sums[i] is None else sums[i] + part * share
        return sums

    def keep(o):
        for i, value in enumerate(combine(o)):
            U[o % Z, i] = value.astype(BF16)

    def relay(d, sg):
        mine = [U[(3 * sg) % Z, i].astype(F32) for i in range(2)]
        for k in range(2):
            wait_for(rr.at[d, k], rsr.at[d, k])
            mine = [mine[i] + rr[d, k, i].astype(F32) for i in range(2)]
        wait_for(rr.at[d, 2, d], rsr.at[d, 2])
        mine[d] = mine[d] + rr[d, 2, d].astype(F32)
        for i in range(2):
            U[(3 * sg) % Z, i] = mine[i].astype(BF16)
        send(U.at[(3 * sg) % Z], rf.at[d, 2], rsz_send, rsf.at[d, 2], 3 * sg, 0)

    keep(6)
    for d, sg in SIDES:
        send(U.at[6, d], rr.at[d, 2, d], rsz_send, rsr.at[d, 2], 3 * sg, 0)
    for k in (1, 0):
        for d, sg in SIDES:
            o = sg * (4 + k)
            keep(o)
            send(U.at[o % Z], rr.at[d, k], rsz_send, rsr.at[d, k], sg * (k + 1), 0)
    for d, sg in SIDES:
        keep(3 * sg)
    for d, sg in SIDES:
        keep(2 * sg)
        send(U.at[(2 * sg) % Z], rf.at[d, 1], rsz_send, rsf.at[d, 1], 2 * sg, 0)
    for d, sg in SIDES:
        relay(d, sg)
    for d, sg in SIDES:
        keep(sg)
        send(U.at[sg % Z], rf.at[d, 0], rsz_send, rsf.at[d, 0], sg, 0)
    last = combine(0)
    for k in range(3):
        for d, sg in SIDES:
            wait_for(rf.at[d, k], rsf.at[d, k])
            last = [last[i] + rf[d, k, i].astype(F32) for i in range(2)]
    for i in range(2):
        kg_ref[i] = last[i][0:blk].astype(BF16)
        vg_ref[i] = last[i][blk:].astype(BF16)

    wait_for(tab.at[0:X - 1], tab_send)
    wait_for(G.at[0:Z - 1], agz_send)
    wait_for(U.at[0:Z - 1], rsz_send)
    wait_for(C.at[0:(X - 1) * (Z + 1)], agx_send)
    wait_for(T.at[0:(X - 1) * Z], rsx_send)
    wait_for(res, pipe_send)
    wait_for(res, pipe_recv)


def write_kernel(recv_ref, kg_ref, vg_ref, next_ref, back_ref, kgo_ref, vgo_ref, zero, sem):
    pipe = lax.axis_index("pipe")
    copies = [
        pltpu.make_async_copy(kg_ref, kgo_ref, sem.at[0]),
        pltpu.make_async_copy(vg_ref, vgo_ref, sem.at[1]),
    ]
    for copy in copies:
        copy.start()

    def finish(got_ref, blank_ref):
        got = pltpu.make_async_copy(recv_ref, got_ref, sem.at[2])
        got.start()
        zero[...] = jnp.zeros_like(zero)
        blank = pltpu.make_async_copy(zero, blank_ref, sem.at[3])
        blank.start()
        got.wait()
        blank.wait()

    @pl.when(pipe == 0)
    def _():
        finish(back_ref, next_ref)

    @pl.when(pipe == 1)
    def _():
        finish(next_ref, back_ref)

    for copy in copies:
        copy.wait()


def local(stream_in, saved_in, grad_out, mem_keys, mem_values, owner_map, block_ids):
    n_blk, blk = mem_keys.shape[1:3]
    picks = block_ids.shape[3]
    tokens, W = stream_in.shape[1:]
    heads = W // HEAD
    keys = picks * blk
    both = 2 * blk
    DMA = pltpu.SemaphoreType.DMA
    anywhere = pl.BlockSpec(memory_space=pl.ANY)
    in_vmem = pl.BlockSpec(memory_space=pltpu.VMEM)
    wide = jax.ShapeDtypeStruct((tokens, W), BF16)
    small = jax.ShapeDtypeStruct((n_blk, blk, W), BF16)
    held = pltpu.VMEM((tokens, W), BF16)
    held_small = pltpu.VMEM((n_blk, blk, W), BF16)
    operands = (
        stream_in[0], saved_in[0], grad_out[0], mem_keys[0], mem_values[0], owner_map, block_ids
    )
    recv, kg, vg = pl.pallas_call(
        functools.partial(main_kernel, blk, picks),
        out_shape=(held, held_small, held_small),
        in_specs=[anywhere] * 7,
        out_specs=(anywhere, in_vmem, in_vmem),
        scratch_shapes=[
            pltpu.VMEM((tokens, W), BF16),
            pltpu.VMEM((tokens, W), BF16),
            pltpu.VMEM((tokens, W), BF16),
            pltpu.VMEM((heads, HEAD, tokens), BF16),
            pltpu.VMEM((heads, HEAD, tokens), BF16),
            pltpu.VMEM((2, n_blk, blk, W), BF16),
            pltpu.VMEM((X, 8, LANES), jnp.int32),
            pltpu.VMEM((Z, 2, both, W), BF16),
            pltpu.VMEM((X - 1, 2, both, W), BF16),
            pltpu.VMEM((X - 1, Z, both, W), BF16),
            pltpu.VMEM((Z * X, both, W), BF16),
            pltpu.VMEM((2, 2 * keys, Z * X * both), BF16),
            pltpu.VMEM((Z * X * both, 2 * keys), BF16),
            pltpu.VMEM((2 * keys, W), BF16),
            pltpu.VMEM((2 * keys, W), BF16),
            pltpu.VMEM((2 * keys, W), BF16),
            pltpu.VMEM((heads, keys, tokens), BF16),
            pltpu.VMEM((tokens, W), BF16),
            pltpu.VMEM((Z * X, both, W), BF16),
            pltpu.VMEM((X - 1, Z, both, W), BF16),
            pltpu.VMEM((Z, 2, both, W), BF16),
            pltpu.VMEM((2, 3, 2, both, W), BF16),
            pltpu.VMEM((2, 3, 2, both, W), BF16),
            pltpu.SMEM(owner_map.shape, jnp.int32),
            pltpu.SMEM(block_ids.shape, jnp.int32),
            pltpu.SMEM((X, 8, LANES), jnp.int32),
            DMA((3,)), DMA((4,)), DMA(()), DMA((X - 1,)), DMA(()),
            DMA((2 * Z,)), DMA((X - 1,)), DMA((X - 1, Z)), DMA(()), DMA(()),
            DMA((X - 1, 2 * Z)), DMA((2, 3)), DMA((2, 3)), DMA(()), DMA(()), DMA(()), DMA(()),
        ],
        compiler_params=pltpu.CompilerParams(
            collective_id=0, has_side_effects=True, vmem_limit_bytes=VMEM_LIMIT
        ),
    )(
        *(pltpu.with_memory_space_constraint(operand, pltpu.HBM) for operand in operands)
    )
    outs = pl.pallas_call(
        write_kernel,
        out_shape=(wide, wide, small, small),
        in_specs=[anywhere] * 3,
        out_specs=(anywhere,) * 4,
        scratch_shapes=[pltpu.VMEM((tokens, W), BF16), DMA((4,))],
        compiler_params=pltpu.CompilerParams(vmem_limit_bytes=VMEM_LIMIT),
    )(recv, kg, vg)
    return tuple(out[None] for out in outs)


def solution(mesh):
    in_specs = (
        P("pipe", "dp", "tensor"),
        P("pipe", "dp", "tensor"),
        P("pipe", "dp", "tensor"),
        P("pipe", "dp", None, "tensor"),
        P("pipe", "dp", None, "tensor"),
        P(),
        P(None, "pipe", "dp", None),
    )
    out_specs = (
        P("pipe", "dp", "tensor"),
        P("pipe", "dp", "tensor"),
        P("pipe", "dp", None, "tensor"),
        P("pipe", "dp", None, "tensor"),
    )
    return jax.shard_map(local, mesh=mesh, in_specs=in_specs, out_specs=out_specs, check_vma=False)
```

```python
import functools
import math

import jax
import jax.numpy as jnp
from jax import lax
from jax.experimental import pallas as pl
from jax.experimental.pallas import tpu as pltpu
from jax.sharding import PartitionSpec as P

HEAD = 128
X = 4
Z = 12
LANES = 128
BF16 = jnp.bfloat16
F32 = jnp.float32
NT = (((1,), (1,)), ((), ()))
TN = (((0,), (0,)), ((), ()))
MESH = pl.DeviceIdType.MESH
SIDES = ((0, 1), (1, -1))
FAR = (6, 5, -5, 4, -4)
VMEM_LIMIT = 40 << 20


def wait_for(ref, sem):
    pltpu.make_async_copy(ref, ref, sem).wait()


def main_kernel(
    blk, picks,
    stream_ref, saved_ref, grad_ref, mk_ref, mv_ref, om_ref, ids_ref,
    recv_ref, kg_ref, vg_ref,
    stream_v, saved_v, grad_v, saved_t, grad_t, mem_v, tab, G, D, S, C, pick, spread, kvb, kvf, terms, gs, res,
    T, rx, U, rr, rf, om_s, ids_s, tab_s,
    load_sem, small_sem, tab_send, tab_recv, tab_sem, agz, agd, agx, agz_send, agx_send,
    rsx, rsr, rsf, rsx_send, rsz_send, pipe_send, pipe_recv,
):
    pipe, dp, ten = lax.axis_index("pipe"), lax.axis_index("dp"), lax.axis_index("tensor")
    z, x = dp // X, dp % X
    W = stream_v.shape[1]
    heads = W // HEAD
    keys = picks * blk
    both = 2 * blk
    total = Z * X * both
    scale = 1.0 / math.sqrt(HEAD)

    def zat(dz):
        return lax.rem(z + dz + Z, Z)

    def at(dz, dx):
        return zat(dz) * X + lax.rem(x + dx + X, X)

    def send(src, dst, ssem, rsem, dz, dx):
        pltpu.make_async_remote_copy(
            src_ref=src, dst_ref=dst, send_sem=ssem, recv_sem=rsem,
            device_id=(pipe, at(dz, dx), ten), device_id_type=MESH,
        ).start()

    mem_loads = [
        pltpu.make_async_copy(mk_ref, mem_v.at[0], small_sem.at[0]),
        pltpu.make_async_copy(mv_ref, mem_v.at[1], small_sem.at[1]),
    ]
    id_loads = [
        pltpu.make_async_copy(om_ref, om_s, small_sem.at[2]),
        pltpu.make_async_copy(ids_ref, ids_s, small_sem.at[3]),
    ]
    loads = [
        pltpu.make_async_copy(saved_ref, saved_v, load_sem.at[0]),
        pltpu.make_async_copy(grad_ref, grad_v, load_sem.at[1]),
        pltpu.make_async_copy(stream_ref, stream_v, load_sem.at[2]),
    ]
    for copy in mem_loads + id_loads:
        copy.start()
    barrier = pltpu.get_barrier_semaphore()
    partners = [(dz, 0) for dz in (3, -3, 2, -2, 1, -1)] + [(0, dx) for dx in range(1, X)]
    for dz, dx in partners:
        pl.semaphore_signal(
            barrier, inc=1, device_id=(pipe, at(dz, dx), ten), device_id_type=MESH
        )
    pl.semaphore_signal(barrier, inc=1, device_id=(1 - pipe, dp, ten), device_id_type=MESH)
    for copy in loads:
        copy.start()

    for copy in mem_loads:
        copy.wait()
    for i in range(2):
        own = jnp.concatenate([mem_v[0, i].astype(F32), mem_v[1, i].astype(F32)], axis=0)
        G[z, i] = own.astype(BF16)

    for copy in id_loads:
        copy.wait()
    places = [[om_s[ids_s[m, 0, 0, j]] for j in range(picks)] for m in range(2)]
    owners = [[place // 2 for place in row] for row in places]
    lane = lax.broadcasted_iota(jnp.int32, (8, LANES), 1)
    wanted = jnp.zeros((8, LANES), jnp.int32)
    for m in range(2):
        for j in range(picks):
            wanted = jnp.where(lane == owners[m][j], places[m][j] % 2, wanted)
    tab[0] = wanted
    pl.semaphore_wait(barrier, len(partners) + 1)

    for dx in range(1, X):
        send(tab.at[0], tab.at[X - dx], tab_send, tab_recv.at[X - dx - 1], 0, dx)
    for dz in (1, -1, 3, -3, 2, -2):
        send(G.at[z], G.at[z], agz_send, agz.at[(-dz) % Z], dz, 0)
    for dx in (2, 1, 3):
        send(G.at[z], D.at[X - dx - 1], agx_send, agd.at[X - dx - 1], 0, dx)

    ramp = lax.broadcasted_iota(jnp.int32, (blk, total), 1) - lax.broadcasted_iota(
        jnp.int32, (blk, total), 0
    )
    for m in (1, 0):
        for kv in range(2):
            for j in range(0, picks, 2):
                pair = [
                    jnp.where(ramp == owners[m][i] * both + kv * blk, 1.0, 0.0).astype(F32)
                    for i in (j, j + 1)
                ]
                row = kv * keys + j * blk
                pick[m, row:row + both, :] = jnp.concatenate(pair, axis=0).astype(BF16)

    for dx in range(1, X):
        wait_for(tab.at[dx], tab_recv.at[dx - 1])
    to_scalars = pltpu.make_async_copy(tab, tab_s, tab_sem)
    to_scalars.start()
    to_scalars.wait()

    def slot(dx, o):
        return tab_s[dx, 0, at(o, 0)]

    def to_peers(o):
        if o == 6:
            for d, _ in SIDES:
                wait_for(G.at[zat(6), d], agz.at[6 + d * Z])
        elif abs(o) != 3:
            wait_for(G.at[zat(o)], agz.at[o % Z])
        first, second = G[zat(o), 0], G[zat(o), 1]
        for dx in (2, 1, 3):
            S[dx - 1, o % Z] = jnp.where(slot(dx, o) == 1, second, first)
            send(
                S.at[dx - 1, o % Z], C.at[at(o, 0)], agx_send, agx.at[X - dx - 1, o % Z], 0, dx
            )
        C[at(o, 0)] = jnp.where(slot(0, o) == 1, second, first)

    to_peers(1)
    to_peers(-1)
    for d, sg in SIDES:
        far = G.at[zat(-3 * sg)]
        wait_for(far, agz.at[(-3 * sg) % Z])
        send(far, far, agz_send, agz.at[(-4 * sg) % Z], sg, 0)
        send(far, far, agz_send, agz.at[(-5 * sg) % Z], 2 * sg, 0)
        part = G.at[zat(-3 * sg), d]
        send(part, part, agz_send, agz.at[6 + d * Z], 3 * sg, 0)
    for o in (3, -3, 2, -2):
        to_peers(o)
    C[dp] = jnp.where(slot(0, 0) == 1, G[z, 1], G[z, 0])
    for dx in range(1, X):
        wait_for(D.at[dx - 1], agd.at[dx - 1])
        mine = tab_s[0, 0, at(0, dx)]
        C[at(0, dx)] = jnp.where(mine == 1, D[dx - 1, 1], D[dx - 1, 0])
    for copy in loads:
        copy.wait()
    for h in range(heads // 2):
        cut = slice(h * HEAD, (h + 1) * HEAD)
        saved_t[h], grad_t[h] = saved_v[:, cut].T, grad_v[:, cut].T
    for o in (4, -4, 5, -5, 6):
        to_peers(o)
    for h in range(heads // 2, heads):
        cut = slice(h * HEAD, (h + 1) * HEAD)
        saved_t[h], grad_t[h] = saved_v[:, cut].T, grad_v[:, cut].T

    column = lax.broadcasted_iota(jnp.int32, (1, 2 * keys), 1)
    target = column % blk + jnp.where(column >= keys, blk, 0)
    for j in range(picks):
        target = target + jnp.where((column % keys) // blk == j, owners[1][j] * both, 0)
    hits = lax.broadcasted_iota(jnp.int32, (total, 2 * keys), 0) == target
    spread[...] = jnp.where(hits, 1.0, 0.0).astype(BF16)

    for o in (1, -1, 3, -3, 2, -2, 4, -4, 5, -5, 6):
        for dx in range(1, X):
            wait_for(C.at[at(o, dx)], agx.at[dx - 1, o % Z])

    def select(m):
        return jnp.dot(
            pick[m], C[...].reshape(total, W), preferred_element_type=F32
        ).astype(BF16)

    def powers(st):
        return jnp.exp2((st - jnp.max(st, axis=0, keepdims=True)) * (scale * math.log2(math.e)))

    def backward_head(h):
        cut = slice(h * HEAD, (h + 1) * HEAD)
        e = powers(jnp.dot(kvb[0:keys, cut], saved_t[h], preferred_element_type=F32))
        gw = jnp.dot(kvb[keys:, cut], grad_t[h], preferred_element_type=F32)
        share = 1.0 / jnp.sum(e, axis=0, keepdims=True)
        centre = jnp.sum(e * gw, axis=0, keepdims=True) * share
        gst = (e * (share * scale) * (gw - centre)).astype(BF16)
        gs[h] = gst
        terms[0:keys, cut] = jnp.dot(
            gst, saved_v[:, cut], preferred_element_type=F32
        ).astype(BF16)
        terms[keys:, cut] = jnp.dot(
            (e * share).astype(BF16), grad_v[:, cut], preferred_element_type=F32
        ).astype(BF16)

    def to_column(o, part):
        index = o % Z if part is None else o % Z + part * Z
        cols = slice(0, W) if part is None else slice(part * W // 2, (part + 1) * W // 2)
        for dx in (2, 1, 3):
            send(
                T.at[at(o, dx), :, cols], rx.at[X - dx - 1, o % Z, :, cols],
                rsx_send, rsx.at[X - dx - 1, index], 0, dx,
            )

    kvb[...] = select(1)
    for part in range(2):
        for h in range(part * heads // 2, (part + 1) * heads // 2):
            backward_head(h)
        cols = slice(part * W // 2, (part + 1) * W // 2)
        T[:, :, cols] = jnp.dot(
            spread[...], terms[:, cols], preferred_element_type=F32
        ).astype(BF16).reshape(Z * X, both, W // 2)
        for o in FAR:
            to_column(o, part)
    for o in (2, -2, 1, -1, 3, -3, 0):
        to_column(o, None)

    def exchange():
        return pltpu.make_async_remote_copy(
            src_ref=res, dst_ref=recv_ref, send_sem=pipe_send, recv_sem=pipe_recv,
            device_id=(1 - pipe, dp, ten), device_id_type=MESH,
        )

    @pl.when(pipe == 0)
    def _():
        kvf[...] = select(0)
        for h in range(heads):
            cut = slice(h * HEAD, (h + 1) * HEAD)
            s_h = stream_v[:, cut]
            e = powers(lax.dot_general(kvf[0:keys, cut], s_h, NT, preferred_element_type=F32))
            w = (e * (1.0 / jnp.sum(e, axis=0, keepdims=True))).astype(BF16)
            out = lax.dot_general(w, kvf[keys:, cut], TN, preferred_element_type=F32)
            res[:, cut] = (s_h.astype(F32) + out).astype(BF16)

    @pl.when(pipe == 1)
    def _():
        for h in range(heads):
            cut = slice(h * HEAD, (h + 1) * HEAD)
            out = lax.dot_general(gs[h], kvb[0:keys, cut], TN, preferred_element_type=F32)
            res[:, cut] = (grad_v[:, cut].astype(F32) + out).astype(BF16)

    exchange().start()

    def combine(o):
        for dx in range(1, X):
            if o in FAR:
                for part in range(2):
                    cols = slice(part * W // 2, (part + 1) * W // 2)
                    wait_for(rx.at[dx - 1, o % Z, :, cols], rsx.at[dx - 1, o % Z + part * Z])
            else:
                wait_for(rx.at[dx - 1, o % Z], rsx.at[dx - 1, o % Z])
        sums = [None, None]
        for dx in range(X):
            part = (T[at(o, 0)] if dx == 0 else rx[dx - 1, o % Z]).astype(F32)
            second = slot(dx, o).astype(F32)
            for i, share in enumerate((1.0 - second, second)):
                sums[i] = part * share if sums[i] is None else sums[i] + part * share
        return sums

    def keep(o):
        for i, value in enumerate(combine(o)):
            U[o % Z, i] = value.astype(BF16)

    def relay(d, sg):
        mine = [U[(3 * sg) % Z, i].astype(F32) for i in range(2)]
        for k in range(2):
            wait_for(rr.at[d, k], rsr.at[d, k])
            mine = [mine[i] + rr[d, k, i].astype(F32) for i in range(2)]
        wait_for(rr.at[d, 2, d], rsr.at[d, 2])
        mine[d] = mine[d] + rr[d, 2, d].astype(F32)
        for i in range(2):
            U[(3 * sg) % Z, i] = mine[i].astype(BF16)
        send(U.at[(3 * sg) % Z], rf.at[d, 2], rsz_send, rsf.at[d, 2], 3 * sg, 0)

    keep(6)
    for d, sg in SIDES:
        send(U.at[6, d], rr.at[d, 2, d], rsz_send, rsr.at[d, 2], 3 * sg, 0)
    for k in (1, 0):
        for d, sg in SIDES:
            o = sg * (4 + k)
            keep(o)
            send(U.at[o % Z], rr.at[d, k], rsz_send, rsr.at[d, k], sg * (k + 1), 0)
    for k in (1, 0):
        for d, sg in SIDES:
            o = sg * (k + 1)
            keep(o)
            send(U.at[o % Z], rf.at[d, k], rsz_send, rsf.at[d, k], o, 0)
    for d, sg in SIDES:
        keep(3 * sg)
    for d, sg in SIDES:
        relay(d, sg)
    last = combine(0)
    for k in range(3):
        for d, sg in SIDES:
            wait_for(rf.at[d, k], rsf.at[d, k])
            last = [last[i] + rf[d, k, i].astype(F32) for i in range(2)]
    for i in range(2):
        kg_ref[i] = last[i][0:blk].astype(BF16)
        vg_ref[i] = last[i][blk:].astype(BF16)

    wait_for(tab.at[0:X - 1], tab_send)
    wait_for(G.at[0:Z - 1], agz_send)
    wait_for(U.at[0:Z - 1], rsz_send)
    wait_for(C.at[0:(X - 1) * (Z + 1)], agx_send)
    wait_for(T.at[0:(X - 1) * Z], rsx_send)
    wait_for(res, pipe_send)
    wait_for(res, pipe_recv)


def write_kernel(recv_ref, kg_ref, vg_ref, next_ref, back_ref, kgo_ref, vgo_ref, zero, sem):
    pipe = lax.axis_index("pipe")
    copies = [
        pltpu.make_async_copy(kg_ref, kgo_ref, sem.at[0]),
        pltpu.make_async_copy(vg_ref, vgo_ref, sem.at[1]),
    ]
    for copy in copies:
        copy.start()

    def finish(got_ref, blank_ref):
        got = pltpu.make_async_copy(recv_ref, got_ref, sem.at[2])
        got.start()
        zero[...] = jnp.zeros_like(zero)
        blank = pltpu.make_async_copy(zero, blank_ref, sem.at[3])
        blank.start()
        got.wait()
        blank.wait()

    @pl.when(pipe == 0)
    def _():
        finish(back_ref, next_ref)

    @pl.when(pipe == 1)
    def _():
        finish(next_ref, back_ref)

    for copy in copies:
        copy.wait()


def local(stream_in, saved_in, grad_out, mem_keys, mem_values, owner_map, block_ids):
    n_blk, blk = mem_keys.shape[1:3]
    picks = block_ids.shape[3]
    tokens, W = stream_in.shape[1:]
    heads = W // HEAD
    keys = picks * blk
    both = 2 * blk
    DMA = pltpu.SemaphoreType.DMA
    anywhere = pl.BlockSpec(memory_space=pl.ANY)
    in_vmem = pl.BlockSpec(memory_space=pltpu.VMEM)
    wide = jax.ShapeDtypeStruct((tokens, W), BF16)
    small = jax.ShapeDtypeStruct((n_blk, blk, W), BF16)
    held = pltpu.VMEM((tokens, W), BF16)
    held_small = pltpu.VMEM((n_blk, blk, W), BF16)
    operands = (
        stream_in[0], saved_in[0], grad_out[0], mem_keys[0], mem_values[0], owner_map, block_ids
    )
    recv, kg, vg = pl.pallas_call(
        functools.partial(main_kernel, blk, picks),
        out_shape=(held, held_small, held_small),
        in_specs=[anywhere] * 7,
        out_specs=(anywhere, in_vmem, in_vmem),
        scratch_shapes=[
            pltpu.VMEM((tokens, W), BF16),
            pltpu.VMEM((tokens, W), BF16),
            pltpu.VMEM((tokens, W), BF16),
            pltpu.VMEM((heads, HEAD, tokens), BF16),
            pltpu.VMEM((heads, HEAD, tokens), BF16),
            pltpu.VMEM((2, n_blk, blk, W), BF16),
            pltpu.VMEM((X, 8, LANES), jnp.int32),
            pltpu.VMEM((Z, 2, both, W), BF16),
            pltpu.VMEM((X - 1, 2, both, W), BF16),
            pltpu.VMEM((X - 1, Z, both, W), BF16),
            pltpu.VMEM((Z * X, both, W), BF16),
            pltpu.VMEM((2, 2 * keys, Z * X * both), BF16),
            pltpu.VMEM((Z * X * both, 2 * keys), BF16),
            pltpu.VMEM((2 * keys, W), BF16),
            pltpu.VMEM((2 * keys, W), BF16),
            pltpu.VMEM((2 * keys, W), BF16),
            pltpu.VMEM((heads, keys, tokens), BF16),
            pltpu.VMEM((tokens, W), BF16),
            pltpu.VMEM((Z * X, both, W), BF16),
            pltpu.VMEM((X - 1, Z, both, W), BF16),
            pltpu.VMEM((Z, 2, both, W), BF16),
            pltpu.VMEM((2, 3, 2, both, W), BF16),
            pltpu.VMEM((2, 3, 2, both, W), BF16),
            pltpu.SMEM(owner_map.shape, jnp.int32),
            pltpu.SMEM(block_ids.shape, jnp.int32),
            pltpu.SMEM((X, 8, LANES), jnp.int32),
            DMA((3,)), DMA((4,)), DMA(()), DMA((X - 1,)), DMA(()),
            DMA((2 * Z,)), DMA((X - 1,)), DMA((X - 1, Z)), DMA(()), DMA(()),
            DMA((X - 1, 2 * Z)), DMA((2, 3)), DMA((2, 3)), DMA(()), DMA(()), DMA(()), DMA(()),
        ],
        compiler_params=pltpu.CompilerParams(
            collective_id=0, has_side_effects=True, vmem_limit_bytes=VMEM_LIMIT
        ),
    )(
        *(pltpu.with_memory_space_constraint(operand, pltpu.HBM) for operand in operands)
    )
    outs = pl.pallas_call(
        write_kernel,
        out_shape=(wide, wide, small, small),
        in_specs=[anywhere] * 3,
        out_specs=(anywhere,) * 4,
        scratch_shapes=[pltpu.VMEM((tokens, W), BF16), DMA((4,))],
        compiler_params=pltpu.CompilerParams(vmem_limit_bytes=VMEM_LIMIT),
    )(recv, kg, vg)
    return tuple(out[None] for out in outs)


def solution(mesh):
    in_specs = (
        P("pipe", "dp", "tensor"),
        P("pipe", "dp", "tensor"),
        P("pipe", "dp", "tensor"),
        P("pipe", "dp", None, "tensor"),
        P("pipe", "dp", None, "tensor"),
        P(),
        P(None, "pipe", "dp", None),
    )
    out_specs = (
        P("pipe", "dp", "tensor"),
        P("pipe", "dp", "tensor"),
        P("pipe", "dp", None, "tensor"),
        P("pipe", "dp", None, "tensor"),
    )
    return jax.shard_map(local, mesh=mesh, in_specs=in_specs, out_specs=out_specs, check_vma=False)
```

```python
import functools
import math

import jax
import jax.numpy as jnp
from jax import lax
from jax.experimental import pallas as pl
from jax.experimental.pallas import tpu as pltpu
from jax.sharding import PartitionSpec as P

HEAD = 128
X = 4
Z = 12
LANES = 128
BF16 = jnp.bfloat16
F32 = jnp.float32
NT = (((1,), (1,)), ((), ()))
TN = (((0,), (0,)), ((), ()))
MESH = pl.DeviceIdType.MESH
SIDES = ((0, 1), (1, -1))
FAR = (6, 5, -5, 4, -4)
VMEM_LIMIT = 40 << 20


def wait_for(ref, sem):
    pltpu.make_async_copy(ref, ref, sem).wait()


def main_kernel(
    blk, picks,
    stream_ref, saved_ref, grad_ref, mk_ref, mv_ref, om_ref, ids_ref,
    recv_ref, kg_ref, vg_ref,
    stream_v, saved_v, grad_v, saved_t, grad_t, mem_v, tab, G, D, S, C, pick, spread, kvb, kvf, terms, gs, res,
    T, rx, U, rr, rf, om_s, ids_s, tab_s,
    load_sem, small_sem, tab_send, tab_recv, tab_sem, agz, agd, agx, agz_send, agx_send,
    rsx, rsr, rsf, rsx_send, rsz_send, pipe_send, pipe_recv,
):
    pipe, dp, ten = lax.axis_index("pipe"), lax.axis_index("dp"), lax.axis_index("tensor")
    z, x = dp // X, dp % X
    W = stream_v.shape[1]
    heads = W // HEAD
    keys = picks * blk
    both = 2 * blk
    total = Z * X * both
    scale = 1.0 / math.sqrt(HEAD)

    def zat(dz):
        return lax.rem(z + dz + Z, Z)

    def at(dz, dx):
        return zat(dz) * X + lax.rem(x + dx + X, X)

    def send(src, dst, ssem, rsem, dz, dx):
        pltpu.make_async_remote_copy(
            src_ref=src, dst_ref=dst, send_sem=ssem, recv_sem=rsem,
            device_id=(pipe, at(dz, dx), ten), device_id_type=MESH,
        ).start()

    mem_loads = [
        pltpu.make_async_copy(mk_ref, mem_v.at[0], small_sem.at[0]),
        pltpu.make_async_copy(mv_ref, mem_v.at[1], small_sem.at[1]),
    ]
    id_loads = [
        pltpu.make_async_copy(om_ref, om_s, small_sem.at[2]),
        pltpu.make_async_copy(ids_ref, ids_s, small_sem.at[3]),
    ]
    loads = [
        pltpu.make_async_copy(saved_ref, saved_v, load_sem.at[0]),
        pltpu.make_async_copy(grad_ref, grad_v, load_sem.at[1]),
        pltpu.make_async_copy(stream_ref, stream_v, load_sem.at[2]),
    ]
    for copy in mem_loads + id_loads:
        copy.start()
    barrier = pltpu.get_barrier_semaphore()
    partners = [(dz, 0) for dz in (3, -3, 2, -2, 1, -1)] + [(0, dx) for dx in range(1, X)]
    for dz, dx in partners:
        pl.semaphore_signal(
            barrier, inc=1, device_id=(pipe, at(dz, dx), ten), device_id_type=MESH
        )
    pl.semaphore_signal(barrier, inc=1, device_id=(1 - pipe, dp, ten), device_id_type=MESH)
    for copy in loads:
        copy.start()

    for copy in mem_loads:
        copy.wait()
    for i in range(2):
        own = jnp.concatenate([mem_v[0, i].astype(F32), mem_v[1, i].astype(F32)], axis=0)
        G[z, i] = own.astype(BF16)

    for copy in id_loads:
        copy.wait()
    places = [[om_s[ids_s[m, 0, 0, j]] for j in range(picks)] for m in range(2)]
    owners = [[place // 2 for place in row] for row in places]
    lane = lax.broadcasted_iota(jnp.int32, (8, LANES), 1)
    wanted = jnp.zeros((8, LANES), jnp.int32)
    for m in range(2):
        for j in range(picks):
            wanted = jnp.where(lane == owners[m][j], places[m][j] % 2, wanted)
    tab[0] = wanted
    pl.semaphore_wait(barrier, len(partners) + 1)

    for dx in range(1, X):
        send(tab.at[0], tab.at[X - dx], tab_send, tab_recv.at[X - dx - 1], 0, dx)
    for dz in (3, -3, 1, -1, 2, -2):
        send(G.at[z], G.at[z], agz_send, agz.at[(-dz) % Z], dz, 0)
    for dx in (2, 1, 3):
        send(G.at[z], D.at[X - dx - 1], agx_send, agd.at[X - dx - 1], 0, dx)

    ramp = lax.broadcasted_iota(jnp.int32, (blk, total), 1) - lax.broadcasted_iota(
        jnp.int32, (blk, total), 0
    )
    for m in (1, 0):
        for kv in range(2):
            for j in range(0, picks, 2):
                pair = [
                    jnp.where(ramp == owners[m][i] * both + kv * blk, 1.0, 0.0).astype(F32)
                    for i in (j, j + 1)
                ]
                row = kv * keys + j * blk
                pick[m, row:row + both, :] = jnp.concatenate(pair, axis=0).astype(BF16)

    for dx in range(1, X):
        wait_for(tab.at[dx], tab_recv.at[dx - 1])
    to_scalars = pltpu.make_async_copy(tab, tab_s, tab_sem)
    to_scalars.start()
    to_scalars.wait()

    def slot(dx, o):
        return tab_s[dx, 0, at(o, 0)]

    def to_peers(o):
        if o == 6:
            for d, _ in SIDES:
                wait_for(G.at[zat(6), d], agz.at[6 + d * Z])
        elif abs(o) != 3:
            wait_for(G.at[zat(o)], agz.at[o % Z])
        first, second = G[zat(o), 0], G[zat(o), 1]
        for dx in (2, 1, 3):
            S[dx - 1, o % Z] = jnp.where(slot(dx, o) == 1, second, first)
            send(
                S.at[dx - 1, o % Z], C.at[at(o, 0)], agx_send, agx.at[X - dx - 1, o % Z], 0, dx
            )
        C[at(o, 0)] = jnp.where(slot(0, o) == 1, second, first)

    for d, sg in SIDES:
        far = G.at[zat(-3 * sg)]
        wait_for(far, agz.at[(-3 * sg) % Z])
        send(far, far, agz_send, agz.at[(-4 * sg) % Z], sg, 0)
        send(far, far, agz_send, agz.at[(-5 * sg) % Z], 2 * sg, 0)
        part = G.at[zat(-3 * sg), d]
        send(part, part, agz_send, agz.at[6 + d * Z], 3 * sg, 0)
    to_peers(1)
    to_peers(-1)
    for o in (3, -3, 2, -2):
        to_peers(o)
    C[dp] = jnp.where(slot(0, 0) == 1, G[z, 1], G[z, 0])
    for dx in range(1, X):
        wait_for(D.at[dx - 1], agd.at[dx - 1])
        mine = tab_s[0, 0, at(0, dx)]
        C[at(0, dx)] = jnp.where(mine == 1, D[dx - 1, 1], D[dx - 1, 0])
    for copy in loads:
        copy.wait()
    for h in range(heads // 2):
        cut = slice(h * HEAD, (h + 1) * HEAD)
        saved_t[h], grad_t[h] = saved_v[:, cut].T, grad_v[:, cut].T
    for o in (4, -4, 5, -5, 6):
        to_peers(o)
    for h in range(heads // 2, heads):
        cut = slice(h * HEAD, (h + 1) * HEAD)
        saved_t[h], grad_t[h] = saved_v[:, cut].T, grad_v[:, cut].T

    column = lax.broadcasted_iota(jnp.int32, (1, 2 * keys), 1)
    target = column % blk + jnp.where(column >= keys, blk, 0)
    for j in range(picks):
        target = target + jnp.where((column % keys) // blk == j, owners[1][j] * both, 0)
    hits = lax.broadcasted_iota(jnp.int32, (total, 2 * keys), 0) == target
    spread[...] = jnp.where(hits, 1.0, 0.0).astype(BF16)

    for o in (1, -1, 3, -3, 2, -2, 4, -4, 5, -5, 6):
        for dx in range(1, X):
            wait_for(C.at[at(o, dx)], agx.at[dx - 1, o % Z])

    def select(m):
        return jnp.dot(
            pick[m], C[...].reshape(total, W), preferred_element_type=F32
        ).astype(BF16)

    def powers(st):
        return jnp.exp2((st - jnp.max(st, axis=0, keepdims=True)) * (scale * math.log2(math.e)))

    def backward_head(h):
        cut = slice(h * HEAD, (h + 1) * HEAD)
        e = powers(jnp.dot(kvb[0:keys, cut], saved_t[h], preferred_element_type=F32))
        gw = jnp.dot(kvb[keys:, cut], grad_t[h], preferred_element_type=F32)
        share = 1.0 / jnp.sum(e, axis=0, keepdims=True)
        centre = jnp.sum(e * gw, axis=0, keepdims=True) * share
        gst = (e * (share * scale) * (gw - centre)).astype(BF16)
        gs[h] = gst
        terms[0:keys, cut] = jnp.dot(
            gst, saved_v[:, cut], preferred_element_type=F32
        ).astype(BF16)
        terms[keys:, cut] = jnp.dot(
            (e * share).astype(BF16), grad_v[:, cut], preferred_element_type=F32
        ).astype(BF16)

    def to_column(o, part):
        index = o % Z if part is None else o % Z + part * Z
        cols = slice(0, W) if part is None else slice(part * W // 2, (part + 1) * W // 2)
        for dx in (2, 1, 3):
            send(
                T.at[at(o, dx), :, cols], rx.at[X - dx - 1, o % Z, :, cols],
                rsx_send, rsx.at[X - dx - 1, index], 0, dx,
            )

    kvb[...] = select(1)
    for part in range(2):
        for h in range(part * heads // 2, (part + 1) * heads // 2):
            backward_head(h)
        cols = slice(part * W // 2, (part + 1) * W // 2)
        T[:, :, cols] = jnp.dot(
            spread[...], terms[:, cols], preferred_element_type=F32
        ).astype(BF16).reshape(Z * X, both, W // 2)
        for o in FAR:
            to_column(o, part)
    for o in (2, -2, 1, -1, 3, -3, 0):
        to_column(o, None)

    def exchange():
        return pltpu.make_async_remote_copy(
            src_ref=res, dst_ref=recv_ref, send_sem=pipe_send, recv_sem=pipe_recv,
            device_id=(1 - pipe, dp, ten), device_id_type=MESH,
        )

    @pl.when(pipe == 0)
    def _():
        kvf[...] = select(0)
        for h in range(heads):
            cut = slice(h * HEAD, (h + 1) * HEAD)
            s_h = stream_v[:, cut]
            e = powers(lax.dot_general(kvf[0:keys, cut], s_h, NT, preferred_element_type=F32))
            w = (e * (1.0 / jnp.sum(e, axis=0, keepdims=True))).astype(BF16)
            out = lax.dot_general(w, kvf[keys:, cut], TN, preferred_element_type=F32)
            res[:, cut] = (s_h.astype(F32) + out).astype(BF16)

    @pl.when(pipe == 1)
    def _():
        for h in range(heads):
            cut = slice(h * HEAD, (h + 1) * HEAD)
            out = lax.dot_general(gs[h], kvb[0:keys, cut], TN, preferred_element_type=F32)
            res[:, cut] = (grad_v[:, cut].astype(F32) + out).astype(BF16)

    exchange().start()

    def combine(o):
        for dx in range(1, X):
            if o in FAR:
                for part in range(2):
                    cols = slice(part * W // 2, (part + 1) * W // 2)
                    wait_for(rx.at[dx - 1, o % Z, :, cols], rsx.at[dx - 1, o % Z + part * Z])
            else:
                wait_for(rx.at[dx - 1, o % Z], rsx.at[dx - 1, o % Z])
        sums = [None, None]
        for dx in range(X):
            part = (T[at(o, 0)] if dx == 0 else rx[dx - 1, o % Z]).astype(F32)
            second = slot(dx, o).astype(F32)
            for i, share in enumerate((1.0 - second, second)):
                sums[i] = part * share if sums[i] is None else sums[i] + part * share
        return sums

    def keep(o):
        for i, value in enumerate(combine(o)):
            U[o % Z, i] = value.astype(BF16)

    def relay(d, sg):
        mine = [U[(3 * sg) % Z, i].astype(F32) for i in range(2)]
        for k in range(2):
            wait_for(rr.at[d, k], rsr.at[d, k])
            mine = [mine[i] + rr[d, k, i].astype(F32) for i in range(2)]
        wait_for(rr.at[d, 2, d], rsr.at[d, 2])
        mine[d] = mine[d] + rr[d, 2, d].astype(F32)
        for i in range(2):
            U[(3 * sg) % Z, i] = mine[i].astype(BF16)
        send(U.at[(3 * sg) % Z], rf.at[d, 2], rsz_send, rsf.at[d, 2], 3 * sg, 0)

    keep(6)
    for d, sg in SIDES:
        send(U.at[6, d], rr.at[d, 2, d], rsz_send, rsr.at[d, 2], 3 * sg, 0)
    for k in (1, 0):
        for d, sg in SIDES:
            o = sg * (4 + k)
            keep(o)
            send(U.at[o % Z], rr.at[d, k], rsz_send, rsr.at[d, k], sg * (k + 1), 0)
    for k in (1, 0):
        for d, sg in SIDES:
            o = sg * (k + 1)
            keep(o)
            send(U.at[o % Z], rf.at[d, k], rsz_send, rsf.at[d, k], o, 0)
    for d, sg in SIDES:
        keep(3 * sg)
    for d, sg in SIDES:
        relay(d, sg)
    last = combine(0)
    for k in range(3):
        for d, sg in SIDES:
            wait_for(rf.at[d, k], rsf.at[d, k])
            last = [last[i] + rf[d, k, i].astype(F32) for i in range(2)]
    for i in range(2):
        kg_ref[i] = last[i][0:blk].astype(BF16)
        vg_ref[i] = last[i][blk:].astype(BF16)

    wait_for(tab.at[0:X - 1], tab_send)
    wait_for(G.at[0:Z - 1], agz_send)
    wait_for(U.at[0:Z - 1], rsz_send)
    wait_for(C.at[0:(X - 1) * (Z + 1)], agx_send)
    wait_for(T.at[0:(X - 1) * Z], rsx_send)
    wait_for(res, pipe_send)
    wait_for(res, pipe_recv)


def write_kernel(recv_ref, kg_ref, vg_ref, next_ref, back_ref, kgo_ref, vgo_ref, zero, sem):
    pipe = lax.axis_index("pipe")
    copies = [
        pltpu.make_async_copy(kg_ref, kgo_ref, sem.at[0]),
        pltpu.make_async_copy(vg_ref, vgo_ref, sem.at[1]),
    ]
    for copy in copies:
        copy.start()

    def finish(got_ref, blank_ref):
        got = pltpu.make_async_copy(recv_ref, got_ref, sem.at[2])
        got.start()
        zero[...] = jnp.zeros_like(zero)
        blank = pltpu.make_async_copy(zero, blank_ref, sem.at[3])
        blank.start()
        got.wait()
        blank.wait()

    @pl.when(pipe == 0)
    def _():
        finish(back_ref, next_ref)

    @pl.when(pipe == 1)
    def _():
        finish(next_ref, back_ref)

    for copy in copies:
        copy.wait()


def local(stream_in, saved_in, grad_out, mem_keys, mem_values, owner_map, block_ids):
    n_blk, blk = mem_keys.shape[1:3]
    picks = block_ids.shape[3]
    tokens, W = stream_in.shape[1:]
    heads = W // HEAD
    keys = picks * blk
    both = 2 * blk
    DMA = pltpu.SemaphoreType.DMA
    anywhere = pl.BlockSpec(memory_space=pl.ANY)
    in_vmem = pl.BlockSpec(memory_space=pltpu.VMEM)
    wide = jax.ShapeDtypeStruct((tokens, W), BF16)
    small = jax.ShapeDtypeStruct((n_blk, blk, W), BF16)
    held = pltpu.VMEM((tokens, W), BF16)
    held_small = pltpu.VMEM((n_blk, blk, W), BF16)
    operands = (
        stream_in[0], saved_in[0], grad_out[0], mem_keys[0], mem_values[0], owner_map, block_ids
    )
    recv, kg, vg = pl.pallas_call(
        functools.partial(main_kernel, blk, picks),
        out_shape=(held, held_small, held_small),
        in_specs=[anywhere] * 7,
        out_specs=(anywhere, in_vmem, in_vmem),
        scratch_shapes=[
            pltpu.VMEM((tokens, W), BF16),
            pltpu.VMEM((tokens, W), BF16),
            pltpu.VMEM((tokens, W), BF16),
            pltpu.VMEM((heads, HEAD, tokens), BF16),
            pltpu.VMEM((heads, HEAD, tokens), BF16),
            pltpu.VMEM((2, n_blk, blk, W), BF16),
            pltpu.VMEM((X, 8, LANES), jnp.int32),
            pltpu.VMEM((Z, 2, both, W), BF16),
            pltpu.VMEM((X - 1, 2, both, W), BF16),
            pltpu.VMEM((X - 1, Z, both, W), BF16),
            pltpu.VMEM((Z * X, both, W), BF16),
            pltpu.VMEM((2, 2 * keys, Z * X * both), BF16),
            pltpu.VMEM((Z * X * both, 2 * keys), BF16),
            pltpu.VMEM((2 * keys, W), BF16),
            pltpu.VMEM((2 * keys, W), BF16),
            pltpu.VMEM((2 * keys, W), BF16),
            pltpu.VMEM((heads, keys, tokens), BF16),
            pltpu.VMEM((tokens, W), BF16),
            pltpu.VMEM((Z * X, both, W), BF16),
            pltpu.VMEM((X - 1, Z, both, W), BF16),
            pltpu.VMEM((Z, 2, both, W), BF16),
            pltpu.VMEM((2, 3, 2, both, W), BF16),
            pltpu.VMEM((2, 3, 2, both, W), BF16),
            pltpu.SMEM(owner_map.shape, jnp.int32),
            pltpu.SMEM(block_ids.shape, jnp.int32),
            pltpu.SMEM((X, 8, LANES), jnp.int32),
            DMA((3,)), DMA((4,)), DMA(()), DMA((X - 1,)), DMA(()),
            DMA((2 * Z,)), DMA((X - 1,)), DMA((X - 1, Z)), DMA(()), DMA(()),
            DMA((X - 1, 2 * Z)), DMA((2, 3)), DMA((2, 3)), DMA(()), DMA(()), DMA(()), DMA(()),
        ],
        compiler_params=pltpu.CompilerParams(
            collective_id=0, has_side_effects=True, vmem_limit_bytes=VMEM_LIMIT
        ),
    )(
        *(pltpu.with_memory_space_constraint(operand, pltpu.HBM) for operand in operands)
    )
    outs = pl.pallas_call(
        write_kernel,
        out_shape=(wide, wide, small, small),
        in_specs=[anywhere] * 3,
        out_specs=(anywhere,) * 4,
        scratch_shapes=[pltpu.VMEM((tokens, W), BF16), DMA((4,))],
        compiler_params=pltpu.CompilerParams(vmem_limit_bytes=VMEM_LIMIT),
    )(recv, kg, vg)
    return tuple(out[None] for out in outs)


def solution(mesh):
    in_specs = (
        P("pipe", "dp", "tensor"),
        P("pipe", "dp", "tensor"),
        P("pipe", "dp", "tensor"),
        P("pipe", "dp", None, "tensor"),
        P("pipe", "dp", None, "tensor"),
        P(),
        P(None, "pipe", "dp", None),
    )
    out_specs = (
        P("pipe", "dp", "tensor"),
        P("pipe", "dp", "tensor"),
        P("pipe", "dp", None, "tensor"),
        P("pipe", "dp", None, "tensor"),
    )
    return jax.shard_map(local, mesh=mesh, in_specs=in_specs, out_specs=out_specs, check_vma=False)
```
